256 devices in a mesh: gx: 8 (over z), gy: 32 (over y, x, core).
Axes of the slice: x: 4, y: 4, z: 8, core: 2. Of those that a mesh axis runs over, the one named last changes fastest.
Arguments:
- queries: bfloat16 [4096, 4096], P('gy', 'gx'), may hold values from -8 to 8
- new_kv: bfloat16 [4096, 8, 128], P('gy', 'gx'), may hold values from -8 to 8
- kv_cache: bfloat16 [16384, 8, 128], P('gy', 'gx'), may hold values from -8 to 8
- cache_seg: int32 [16384], P('gy'), may hold values from -1 to 15, as said below
- cache_slot: int32 [4096], P('gy'), may hold values from 0 to 16383, as said below
- token_seg: int32 [4096], P('gy'), may hold values from 0 to 15, never falling along the last dimension, each value on 1 to 2048 neighbouring positions
- pad_mask: int32 [4096], P('gy'), may hold values 0 or 1
- sink_logits: float32 [64], P('gx'), may hold values from 0 to 4
- out_weight: bfloat16 [4096, 2880], P('gx', 'gy'), may hold values from -0.75 to 0.75
- out_bias: float32 [2880], P('gx'), may hold values from -2 to 2
Outputs:
- attended: bfloat16 [4096, 2880], P('gy', 'gx')
- cache_out: bfloat16 [16384, 8, 128], P('gy', 'gx')
The draws below stay inside these ranges and needn't reach their ends.
Inputs may be any that keep to these rules, and one draw needn't show every extreme that they name: `cache_seg`: the sequence whose cached key and value a slot holds, or -1 for an empty slot. Distinct slots, each empty (-1) in cache_seg; cache_slot[t] // 512 == t // 128.
All inputs are finite; a program needn't handle non-finite values. No bound on the sum of `pad_mask` on one device may be relied on, other than what follows from the above.
Results may differ from the reference program's by a relative error of at most 0.015.
Values may be sent and summed in bfloat16 or wider, within the bound.
A program may use at most 128 MiB of HBM per device.

```python
import math
import jax
import jax.numpy as jnp
import numpy as np
from jax import lax

D = 2880
HEADS = 64
KVH = 8
HD = 64
TOK_DEV = 128
CACHE_DEV = 512
NSEG = 16
TOKENS = 4096
CACHE = 16384
LONG = 2048


def draw_queries(key, part):
    values = jax.random.truncated_normal(jax.random.fold_in(key, 11), -8.0, 8.0, (TOKENS, HEADS, HD), jnp.float32)
    return values.reshape(TOKENS, HEADS * HD).astype(jnp.bfloat16)


def draw_new_kv(key, part):
    values = jax.random.truncated_normal(jax.random.fold_in(key, 13), -8.0, 8.0, (TOKENS, KVH, 2 * HD), jnp.float32)
    return values.astype(jnp.bfloat16)


def slot_perms(key):
    shard_count = CACHE // CACHE_DEV
    base = jax.random.fold_in(key, 202)
    shard_keys = jax.random.split(base, shard_count)
    return jax.vmap(lambda one_key: jax.random.permutation(one_key, CACHE_DEV))(shard_keys).astype(jnp.int32)


def draw_cache_slot(key, part):
    shard_count = CACHE // CACHE_DEV
    perms = slot_perms(key)
    offsets = jnp.arange(shard_count, dtype=jnp.int32)[:, None] * CACHE_DEV
    return (perms[:, :TOK_DEV] + offsets).reshape(TOKENS).astype(jnp.int32)


def draw_cache_seg(key, part):
    shard_count = CACHE // CACHE_DEV
    perms = slot_perms(key)
    ranks = jnp.argsort(perms, axis=1, stable=True)
    writes = ranks < TOK_DEV
    first_owner = jax.random.randint(jax.random.fold_in(key, 205), (shard_count, CACHE_DEV), 0, NSEG)
    second_owner = jax.random.randint(jax.random.fold_in(key, 206), (shard_count, CACHE_DEV), 0, NSEG)
    owner = jnp.minimum(first_owner, second_owner)
    empty = jax.random.randint(jax.random.fold_in(key, 207), (shard_count, CACHE_DEV), 0, 8) == 0
    return jnp.where(writes | empty, -1, owner).reshape(CACHE).astype(jnp.int32)


def touch_ends(result, key, smallest, top_value):
    place = [jax.random.randint(jax.random.fold_in(key, axis), (), 0, length) for axis, length in enumerate(result.shape)]
    longest = result.shape.index(max(result.shape))
    next_to = place[:longest] + [(place[longest] + 1) % result.shape[longest]] + place[longest + 1:]
    return result.at[tuple(place)].set(smallest).at[tuple(next_to)].set(top_value)


def levels(key, dims, cuts, least, largest):
    loudness, own = 1.0, jax.random.fold_in(key, 6)
    for position, shards_of in cuts:
        draws = jnp.exp(jax.random.uniform(jax.random.fold_in(own, position), (shards_of,), jnp.float32, least / len(cuts), largest / len(cuts)))
        loudness = loudness * jnp.repeat(draws, dims[position] // shards_of).reshape([-1 if axis == position else 1 for axis in range(len(dims))])
    return loudness


def split_up(number_of, total, reach, lean):
    weights = [(1 << 20) // math.isqrt(grade ** lean) + 1 for grade in range(2, number_of + 1)]
    spare, counts = total - reach - (number_of - 1), [1] * (number_of - 1)
    while spare > 0:
        free = [i for i in range(number_of - 1) if counts[i] < reach]
        pool, remaining = sum([weights[i] for i in free]), spare
        for i in free:
            addition = min(reach - counts[i], max(1, remaining * weights[i] // pool), spare)
            counts[i] = counts[i] + addition
            spare = spare - addition
    return np.array([reach] + counts)


def ragged(rng, count, total, reach, skew):
    if count == 2:
        one = jax.random.randint(rng, (), max(1, total - reach), min(reach, total - 1) + 1)
        return jnp.stack([one, total - one])
    lengths = jnp.asarray(split_up(count, total, reach, skew), jnp.int32)
    pairs = (count - 1) // 2
    giver, sink = lengths[1:1 + 2 * pairs:2], lengths[2:2 + 2 * pairs:2]
    room = jnp.minimum(giver - 1, reach - sink)
    moved = jax.random.randint(jax.random.fold_in(rng, 1), (pairs,), 0, 1 << 20) % (room + 1)
    lengths = lengths.at[1:1 + 2 * pairs:2].set(giver - moved).at[2:2 + 2 * pairs:2].set(sink + moved)
    return lengths[jax.random.permutation(jax.random.fold_in(rng, 2), count)]


def noise(key, shape, scale, reach, cuts=(), held_as=jnp.bfloat16):
    values = jax.random.normal(key, shape, jnp.float32) * scale
    if len(cuts) > 0:
        values = levels(key, shape, cuts, -0.22, 0.18) * values
    return jnp.clip(values, min=-reach, max=reach).astype(held_as)


def setup_inputs(seed: int = 0) -> dict:
    streams_of = jax.random.split(jax.random.key(seed), 11)
    queries = draw_queries(jax.random.fold_in(streams_of[10], 71), 0)
    new_kv = draw_new_kv(jax.random.fold_in(streams_of[10], 71), 0)
    kv_cache = noise(streams_of[2], (CACHE, KVH, 2 * HD), 1.0, 8.0, ((0, 32), (1, 8)))
    cache_seg = draw_cache_seg(jax.random.fold_in(streams_of[10], 71), 0)
    cache_slot = draw_cache_slot(jax.random.fold_in(streams_of[10], 71), 0)
    token_seg = jnp.searchsorted(jnp.cumsum(ragged(streams_of[5], NSEG, TOKENS, LONG, 2)), jnp.arange(TOKENS), side="right").astype(jnp.int32)
    pad_mask = touch_ends((jax.random.randint(streams_of[6], (TOKENS,), 0, 16) < 15).astype(jnp.int32), jax.random.fold_in(streams_of[6], 1), 0, 1)
    sink_logits = jnp.clip(4.0 * jax.random.uniform(streams_of[7], (HEADS,), jnp.float32) ** levels(streams_of[7], (HEADS,), ((0, 8),), -0.2, 0.2), 0.0, 4.0)
    out_weight = noise(streams_of[8], (HEADS * HD, D), HD ** -0.5, 0.75, ((0, 8), (1, 32)))
    out_bias = noise(streams_of[9], (D,), 0.3, 2.0, ((0, 8),), jnp.float32)
    return dict(queries=queries, new_kv=new_kv, kv_cache=kv_cache, cache_seg=cache_seg, cache_slot=cache_slot, token_seg=token_seg, pad_mask=pad_mask, sink_logits=sink_logits, out_weight=out_weight, out_bias=out_bias)


def reference(queries, new_kv, kv_cache, cache_seg, cache_slot, token_seg, pad_mask, sink_logits, out_weight, out_bias):
    live_rows = pad_mask == 1
    target = jnp.where(live_rows, cache_slot, CACHE).astype(jnp.int32)
    cache_out = kv_cache.at[target].set(new_kv, mode="drop")
    slot_seg = cache_seg.at[target].set(token_seg, mode="drop")
    token_index = jnp.arange(TOKENS, dtype=jnp.int32)
    slot_order = jnp.full((CACHE,), -1, jnp.int32).at[target].set(token_index, mode="drop")
    group_heads = HEADS // KVH
    scale = HD ** -0.5
    keys_all = jnp.transpose(cache_out[:, :, :HD].astype(jnp.float32), (1, 0, 2))
    values_all = jnp.transpose(cache_out[:, :, HD:].astype(jnp.float32), (1, 0, 2))
    query_heads = queries.astype(jnp.float32).reshape(TOKENS, KVH, group_heads, HD)
    sink_table = sink_logits.reshape(KVH, group_heads)
    row_block = math.gcd(TOKENS, 256)

    def one_block(row_start):
        block_queries = lax.dynamic_slice_in_dim(query_heads, row_start, row_block, 0)
        block_seg = lax.dynamic_slice_in_dim(token_seg, row_start, row_block, 0)
        block_index = row_start + jnp.arange(row_block, dtype=jnp.int32)
        visible = (slot_seg[None, :] == block_seg[:, None]) & (slot_order[None, :] <= block_index[:, None])

        def one_group(group_data):
            grp_queries, grp_keys, grp_values, grp_sink = group_data
            scores = jnp.einsum("tqd,cd->qtc", grp_queries, grp_keys) * scale
            sink_col = grp_sink[:, None]
            peak = jnp.maximum(sink_col, jnp.max(jnp.where(visible[None], scores, -jnp.inf), axis=-1))
            weights = jnp.where(visible[None], jnp.exp(scores - peak[..., None]), 0.0)
            rounded = lax.optimization_barrier(weights.astype(jnp.bfloat16)).astype(jnp.float32)
            numerator = jnp.einsum("qtc,cd->tqd", rounded, grp_values)
            denominator = jnp.exp(sink_col - peak) + jnp.sum(weights, axis=-1)
            return numerator / jnp.transpose(denominator)[:, :, None]

        grouped = lax.map(one_group, (jnp.transpose(block_queries, (1, 0, 2, 3)), keys_all, values_all, sink_table))
        return jnp.transpose(grouped, (1, 0, 2, 3)).reshape(row_block, HEADS * HD)

    starts = jnp.arange(TOKENS // row_block, dtype=jnp.int32) * row_block
    blocks = lax.map(one_block, starts).reshape(TOKENS, HEADS * HD)
    attention = (blocks * pad_mask[:, None].astype(jnp.float32)).astype(jnp.bfloat16)
    projected = jnp.dot(attention, out_weight, preferred_element_type=jnp.float32) + out_bias
    return projected.astype(jnp.bfloat16), cache_out
```

```python
import jax
import jax.numpy as jnp
from jax import lax
from jax.experimental import pallas as pl
from jax.experimental.pallas import tpu as pltpu
from jax.sharding import PartitionSpec as P

MESH = pl.DeviceIdType.MESH
F32 = jnp.float32
BF16 = jnp.bfloat16
NX, NY, NC = 4, 4, 2
NBLK = NX * NY * NC
SLOTS = 512
TOK = 128
META = 16
KVROWS = SLOTS + META
WCOLS = 90
WPAD = 96
WROWS = 4 * WPAD
ROWS = KVROWS + WROWS
PENALTY = -1048576.0
VMEM_LIMIT = 60 * 1024 * 1024
NT = (((1,), (1,)), ((), ()))


def iota(shape, axis):
    return lax.broadcasted_iota(jnp.int32, shape, axis)


def to_column(row):
    return jnp.transpose(jnp.broadcast_to(row, (8, row.shape[1])))[:, :1]


def prep_kernel(new_ref, kv_ref, cseg_ref, cslot_ref, tseg_ref, pad_ref, wt_ref, cache_ref, blk_ref, own_ref):
    own = lax.axis_index("gy")
    target = jnp.where(pad_ref[...] == 1, cslot_ref[...] - own * SLOTS, SLOTS)
    target_f = target.astype(F32)
    tseg_f = tseg_ref[...].astype(F32)
    place = (iota((SLOTS, TOK), 0).astype(F32) == target_f).astype(F32)
    place_b = place.astype(BF16)
    hit_col = jnp.sum(place, axis=1, keepdims=True)
    put = jnp.dot(place_b, new_ref[...], preferred_element_type=F32)
    cache = jnp.where(hit_col > 0.5, put, kv_ref[...].astype(F32)).astype(BF16)
    cache_ref[...] = cache
    order = iota((1, TOK), 1).astype(F32) + 1.0
    which = iota((8, TOK), 0)
    facts = jnp.where(which == 0, tseg_f, jnp.where(which == 1, order, jnp.where(which == 2, 1.0, 0.0)))
    spread = lax.dot_general(facts.astype(BF16), place_b, NT, preferred_element_type=F32)
    hit = spread[2:3] > 0.5
    cseg_f = cseg_ref[...].astype(F32)
    key = jnp.where(hit, spread[0:1], jnp.where(cseg_f < 0.0, 16.0, cseg_f))
    ordered = spread[1:2]
    which = iota((8, SLOTS), 0)
    own_ref[...] = jnp.where(which == 0, key, jnp.where(which == 1, ordered, 0.0))
    double = key * 2.0 + jnp.where(hit, 1.0, 0.0)
    unique = double * SLOTS + iota((1, SLOTS), 1).astype(F32)
    unique_col = to_column(unique)
    rank = jnp.sum((unique_col < unique).astype(F32), axis=0, keepdims=True)
    permute = (iota((SLOTS, SLOTS), 0).astype(F32) == rank).astype(BF16)
    blk_ref[:SLOTS, :] = jnp.dot(permute, cache, preferred_element_type=F32).astype(BF16)
    double_col = to_column(double)
    lane_seg = ((iota((1, 128), 1) - 64) * 2).astype(F32)
    start = jnp.sum((double_col < lane_seg).astype(F32), axis=0, keepdims=True)
    middle = jnp.sum((double_col < lane_seg + 1.0).astype(F32), axis=0, keepdims=True)
    end = jnp.sum((double_col < lane_seg + 2.0).astype(F32), axis=0, keepdims=True)
    rows = []
    for value in (start, middle, end):
        high = jnp.where(value >= 512.0, 2.0, jnp.where(value >= 256.0, 1.0, 0.0))
        rows += [value - 256.0 * high, high]
    which = iota((META, 128), 0)
    meta = jnp.zeros((META, 128), F32)
    for i, row in enumerate(rows):
        meta = jnp.where(which == i, row, meta)
    blk_ref[SLOTS:KVROWS, :] = meta.astype(BF16)
    weights = jnp.concatenate([wt_ref[...].astype(F32), jnp.zeros((WPAD - WCOLS, 4 * 128), F32)], axis=0)
    for k in range(4):
        blk_ref[KVROWS + k * WPAD : KVROWS + (k + 1) * WPAD, :] = weights[:, k * 128 : (k + 1) * 128].astype(BF16)


def splits(rows):
    units = rows // 16
    edges = [0]
    for i in range(4):
        edges.append(edges[-1] + 16 * ((units + 3 - i) // 4))
    return edges


def gather_kernel(copies, blk_ref, out_ref, local_sem, send_sem, recv_sem):
    gx = lax.axis_index("gx")
    gy = lax.axis_index("gy")
    core = gy % NC
    x = (gy // NC) % NX
    y = gy // (NC * NX)

    def index(xx, yy, cc):
        return ((yy % NY) * NX + xx % NX) * NC + cc

    xp, xm = index(x + 1, y, core), index(x + 3, y, core)
    yp, ym = index(x, y + 1, core), index(x, y + 3, core)
    mate = index(x, y, 1 - core)
    barrier = pltpu.get_barrier_semaphore()
    for peer in (xp, xm, yp, ym, mate):
        pl.semaphore_signal(barrier, inc=1, device_id=(gx, peer), device_id_type=MESH)
    own = index(x, y, core)
    local = pltpu.make_async_copy(blk_ref, out_ref.at[own], local_sem)
    local.start()
    pl.semaphore_wait(barrier, 5)
    edges = splits(blk_ref.shape[0])
    used = [0]
    started = []
    mates = []

    def send(block, lo, hi, peer, fresh=False):
        slot = used[0]
        used[0] += 1
        rows = pl.ds(lo, hi - lo)
        source = blk_ref.at[rows] if fresh else out_ref.at[block, rows]
        copy = pltpu.make_async_remote_copy(
            src_ref=source,
            dst_ref=out_ref.at[block, rows],
            send_sem=send_sem.at[slot],
            recv_sem=recv_sem.at[slot],
            device_id=(gx, peer),
            device_id_type=MESH,
        )
        copy.start()
        started.append(copy)
        if peer is mate:
            mates.append(copy)
        return copy

    halves = []
    for half in range(2):
        lo, mid, hi = edges[2 * half], edges[2 * half + 1], edges[2 * half + 2]
        if half == 0:
            first, second = (xp, xm), (yp, ym)
            place = lambda i, j: index(x + i, y + j, core)
        else:
            first, second = (yp, ym), (xp, xm)
            place = lambda i, j: index(x + j, y + i, core)
        halves.append((lo, mid, hi, first, second, place))

    near = []
    for lo, mid, hi, first, second, place in halves:
        a = send(own, lo, hi, first[0], True)
        b = send(own, lo, hi, first[1], True)
        near.append((a, b))
    far = [[] for _ in halves]
    for h, (lo, mid, hi, first, second, place) in enumerate(halves):
        c = send(own, lo, hi, second[0], True)
        d = send(own, lo, hi, second[1], True)
        far[h].append((0, lo, mid, hi, c, d))
        send(own, lo, hi, mate, True)
    forward = []
    for h, (lo, mid, hi, first, second, place) in enumerate(halves):
        a, b = near[h]
        a.wait_recv()
        fa = send(place(3, 0), lo, mid, first[0])
        c = send(place(3, 0), lo, hi, second[0])
        d = send(place(3, 0), lo, hi, second[1])
        far[h].append((3, lo, mid, hi, c, d))
        b.wait_recv()
        fb = send(place(1, 0), mid, hi, first[1])
        c = send(place(1, 0), lo, hi, second[0])
        d = send(place(1, 0), lo, hi, second[1])
        far[h].append((1, lo, mid, hi, c, d))
        send(place(3, 0), lo, hi, mate)
        send(place(1, 0), lo, hi, mate)
        forward.append((fa, fb))
    last = []

    def relay(h, entry):
        i, lo, mid, hi, c, d = entry
        _, _, _, _, second, place = halves[h]
        c.wait_recv()
        last.append(send(place(i, 3), lo, mid, second[0]))
        d.wait_recv()
        last.append(send(place(i, 1), mid, hi, second[1]))
        send(place(i, 3), lo, hi, mate)
        send(place(i, 1), lo, hi, mate)

    for h in range(2):
        relay(h, far[h][0])
    pieces = []
    for h, (lo, mid, hi, first, second, place) in enumerate(halves):
        fa, fb = forward[h]
        fa.wait_recv()
        c0 = send(place(2, 0), lo, mid, second[0])
        d0 = send(place(2, 0), lo, mid, second[1])
        fb.wait_recv()
        c1 = send(place(2, 0), mid, hi, second[0])
        d1 = send(place(2, 0), mid, hi, second[1])
        send(place(2, 0), lo, hi, mate)
        pieces.append((c0, d0, c1, d1))
    for e in range(1, 3):
        for h in range(2):
            relay(h, far[h][e])
    for h, (lo, mid, hi, first, second, place) in enumerate(halves):
        c0, d0, c1, d1 = pieces[h]
        c0.wait_recv()
        last.append(send(place(2, 3), lo, mid, second[0]))
        d1.wait_recv()
        last.append(send(place(2, 1), mid, hi, second[1]))
        c1.wait_recv()
        send(place(2, 3), lo, hi, mate)
        d0.wait_recv()
        send(place(2, 1), lo, hi, mate)
    order = [(0, 0), (1, 0), (0, 3), (1, 3), (0, 1), (1, 1), (0, 2), (1, 2)]
    for n, (h, i) in enumerate(order):
        lo, mid, hi, first, second, place = halves[h]
        last[2 * n].wait_recv()
        last[2 * n + 1].wait_recv()
        send(place(i, 2), lo, hi, mate)
    for copy in mates:
        copy.wait_recv()
    for copy in started:
        copy.wait_send()
    local.wait()
    assert used[0] == copies


def attend_kernel(
    sink_ref, tseg_s, q_ref, cache_ref, own_ref, tseg_ref, pad_ref, g_ref,
    out_ref, buf, ka, va, qa, m_ref, acc_ref, bound_v, bound_s, lo_ref, hi_ref, sems,
):
    own_block = lax.axis_index("gy")
    load = pltpu.make_async_copy(g_ref.at[:, pl.ds(0, KVROWS)], buf.at[:, pl.ds(0, KVROWS)], sems.at[0])
    load.start()
    lane = iota((1, 128), 1)
    low = lane < 64
    tseg_col = to_column(tseg_ref[...].astype(F32))
    pad_col = to_column(pad_ref[...].astype(F32))
    seg_hot = (tseg_col == (lane - 64).astype(F32)).astype(F32)
    for pair in range(4):
        two = q_ref[:, pair * 128 : (pair + 1) * 128].astype(F32) * 0.125
        qa[2 * pair * TOK : (2 * pair + 1) * TOK, :] = jnp.where(low, two, seg_hot).astype(BF16)
        qa[(2 * pair + 1) * TOK : (2 * pair + 2) * TOK, :] = jnp.where(low, pltpu.roll(two, 64, 1), seg_hot).astype(BF16)
    position = iota((TOK, 1), 0).astype(F32) + 1.0
    shown = (own_ref[0:1, :] == tseg_col) & (own_ref[1:2, :] <= position)
    bias = jnp.where(shown, 0.0, PENALTY)
    kv = cache_ref[...].astype(F32)
    k_own = jnp.where(low, kv, 0.0).astype(BF16)
    v_own = jnp.where(low, 1.0, kv).astype(BF16)
    for h in range(8):
        rows = slice(h * TOK, (h + 1) * TOK)
        scores = lax.dot_general(qa[rows, :], k_own, NT, preferred_element_type=F32) + bias
        peak = jnp.maximum(jnp.max(scores, axis=1, keepdims=True), sink_ref[h])
        weights = jnp.exp(scores - peak)
        acc = jnp.dot(weights.astype(BF16), v_own, preferred_element_type=F32)
        acc_ref[rows, :] = acc + jnp.where(low, jnp.exp(sink_ref[h] - peak), 0.0)
        m_ref[rows, :] = peak
    load.wait()
    seg_lo, seg_hi = tseg_s[0], tseg_s[TOK - 1]
    for b in range(NBLK):
        meta = buf[b, SLOTS:KVROWS, :].astype(F32)
        start = meta[0:1] + 256.0 * meta[1:2]
        middle = meta[2:3] + 256.0 * meta[3:4]
        end = meta[4:5] + 256.0 * meta[5:6]
        lo_ref[b : b + 1, :] = start.astype(jnp.int32)
        hi_ref[b : b + 1, :] = jnp.where(b < own_block, end, middle).astype(jnp.int32)
    lo_all, hi_all = lo_ref[...], hi_ref[...]
    wide = iota((NBLK, 128), 1)
    begin = jnp.sum(jnp.where(wide == seg_lo + 64, lo_all, 0).astype(F32), axis=1, keepdims=True)
    stop = jnp.sum(jnp.where(wide == seg_hi + 64, hi_all, 0).astype(F32), axis=1, keepdims=True)
    bound_v[...] = jnp.where(wide == 0, begin, jnp.where(wide == 1, stop, 0.0)).astype(jnp.int32)
    fetch = pltpu.make_async_copy(bound_v, bound_s, sems.at[1])
    fetch.start()
    fetch.wait()

    def pack_block(b, off):
        first, stop = bound_s[b, 0], bound_s[b, 1]
        base = (first // 16) * 16
        length = jnp.where((b == own_block) | (stop <= first), 0, stop - base)
        low_row = lo_ref[pl.ds(b, 1), :]
        high_row = hi_ref[pl.ds(b, 1), :]

        def piece(i, carry):
            src = pl.multiple_of(base + 64 * i, 16)
            dst = pl.multiple_of(off + 64 * i, 16)
            row = src + iota((64, 128), 0)
            kv = jnp.where(row < SLOTS, buf[b, pl.ds(src, 64), :].astype(F32), 0.0)
            penalty = jnp.where((row >= low_row) & (row < high_row), 0.0, PENALTY)
            ka[pl.ds(dst, 64), :] = jnp.where(low, kv, penalty).astype(BF16)
            va[pl.ds(dst, 64), :] = jnp.where(low, 1.0, kv).astype(BF16)
            return carry

        lax.fori_loop(0, (length + 63) // 64, piece, 0)
        return off + ((length + 15) // 16) * 16

    total = lax.fori_loop(0, NBLK, pack_block, 0)
    tail = pl.multiple_of(total, 16)
    ka[pl.ds(tail, 512), :] = jnp.broadcast_to(jnp.where(low, 0.0, PENALTY), (512, 128)).astype(BF16)
    va[pl.ds(tail, 512), :] = jnp.broadcast_to(jnp.where(low, 1.0, 0.0), (512, 128)).astype(BF16)

    def chunk(i, carry):
        at = pl.multiple_of(i * 512, 512)
        keys, values = ka[pl.ds(at, 512), :], va[pl.ds(at, 512), :]
        for r in range(4):
            rows = slice(r * 256, (r + 1) * 256)
            scores = lax.dot_general(qa[rows, :], keys, NT, preferred_element_type=F32)
            old = m_ref[rows, :]
            peak = jnp.maximum(old, jnp.max(scores, axis=1, keepdims=True))
            weights = jnp.exp(scores - peak)
            acc = jnp.dot(weights.astype(BF16), values, preferred_element_type=F32)
            acc_ref[rows, :] = acc_ref[rows, :] * jnp.exp(old - peak) + acc
            m_ref[rows, :] = peak
        return carry

    lax.fori_loop(0, (total + 511) // 512, chunk, 0)
    for pair in range(4):
        even = acc_ref[2 * pair * TOK : (2 * pair + 1) * TOK, :]
        odd = acc_ref[(2 * pair + 1) * TOK : (2 * pair + 2) * TOK, :]
        top = jnp.where(low, pltpu.roll(even, 64, 1), odd)
        bottom = jnp.where(low, even, pltpu.roll(odd, 64, 1))
        out_ref[:, pair * 128 : (pair + 1) * 128] = (top / bottom * pad_col).astype(BF16)


def project_kernel(nz, attn_ref, bias_ref, g_ref, out_ref, wbuf, sbuf, rbuf, load_sem, send_sem, recv_sem):
    gx = lax.axis_index("gx")
    gy = lax.axis_index("gy")
    load = pltpu.make_async_copy(g_ref.at[:, pl.ds(KVROWS, WROWS)], wbuf, load_sem)
    load.start()
    barrier = pltpu.get_barrier_semaphore()
    for d in range(1, nz):
        pl.semaphore_signal(barrier, inc=1, device_id=((gx + d) % nz, gy), device_id_type=MESH)
    load.wait()

    def partial(dest):
        parts = []
        for b in range(4):
            total = jnp.zeros((WPAD, TOK), F32)
            for k in range(4):
                total += lax.dot_general(
                    wbuf[dest * 4 + b, k * WPAD : (k + 1) * WPAD, :],
                    attn_ref[:, k * 128 : (k + 1) * 128],
                    NT,
                    preferred_element_type=F32,
                )
            parts.append(total)
        return parts

    def send(d):
        copy = pltpu.make_async_remote_copy(
            src_ref=sbuf.at[d - 1],
            dst_ref=rbuf.at[d - 1],
            send_sem=send_sem.at[d - 1],
            recv_sem=recv_sem.at[d - 1],
            device_id=((gx + d) % nz, gy),
            device_id_type=MESH,
        )
        copy.start()
        return copy

    distances = sorted(range(1, nz), key=lambda d: -min(d, nz - d))
    copies = []
    for n, d in enumerate(distances):
        for b, part in enumerate(partial((gx + d) % nz)):
            sbuf[d - 1, b * WPAD : (b + 1) * WPAD, :] = part.astype(BF16)
        if n == 0:
            pl.semaphore_wait(barrier, nz - 1)
        else:
            copies.append(send(distances[n - 1]))
    parts = partial(gx)
    copies.append(send(distances[-1]))
    bias = jnp.transpose(jnp.broadcast_to(bias_ref[...], (128, bias_ref.shape[1])))
    for copy in copies:
        copy.wait_recv()
    sums = []
    for b in range(4):
        total = parts[b]
        for d in range(1, nz):
            total += rbuf[d - 1, b * WPAD : (b + 1) * WPAD, :].astype(F32)
        sums.append(total[:WCOLS])
    out_ref[...] = (jnp.concatenate(sums, axis=0) + bias).astype(BF16)
    for copy in copies:
        copy.wait_send()


VMEM = pl.BlockSpec(memory_space=pltpu.VMEM)
SMEM = pl.BlockSpec(memory_space=pltpu.SMEM)
ANY = pl.BlockSpec(memory_space=pl.ANY)


def solution(mesh):
    nz = mesh.shape["gx"]
    copies = 76

    def shards(queries, new_kv, kv_cache, cache_seg, cache_slot, token_seg, pad_mask, sink_logits, out_weight, out_bias):
        new2 = new_kv.reshape(TOK, 128)
        kv2 = kv_cache.reshape(SLOTS, 128)
        tseg = token_seg.reshape(1, TOK)
        pad = pad_mask.reshape(1, TOK)
        cache_out, block, own = pl.pallas_call(
            prep_kernel,
            name="prep",
            out_shape=(
                jax.ShapeDtypeStruct((SLOTS, 128), BF16),
                jax.ShapeDtypeStruct((ROWS, 128), BF16),
                jax.ShapeDtypeStruct((8, SLOTS), F32),
            ),
            in_specs=[VMEM] * 7,
            out_specs=(VMEM,) * 3,
            compiler_params=pltpu.CompilerParams(vmem_limit_bytes=VMEM_LIMIT),
        )(new2, kv2, cache_seg.reshape(1, SLOTS), cache_slot.reshape(1, TOK), tseg, pad, out_weight.T)
        gathered = pl.pallas_call(
            lambda *refs: gather_kernel(copies, *refs),
            name="gather",
            out_shape=jax.ShapeDtypeStruct((NBLK, ROWS, 128), BF16),
            in_specs=[VMEM],
            out_specs=ANY,
            scratch_shapes=[
                pltpu.SemaphoreType.DMA,
                pltpu.SemaphoreType.DMA((copies,)),
                pltpu.SemaphoreType.DMA((copies,)),
            ],
            compiler_params=pltpu.CompilerParams(collective_id=0, has_side_effects=True),
        )(block)
        attention = pl.pallas_call(
            attend_kernel,
            name="attend",
            out_shape=jax.ShapeDtypeStruct((TOK, 512), BF16),
            in_specs=[SMEM, SMEM, VMEM, VMEM, VMEM, VMEM, VMEM, ANY],
            out_specs=VMEM,
            scratch_shapes=[
                pltpu.VMEM((NBLK, SLOTS + 80, 128), BF16),
                pltpu.VMEM((NBLK * SLOTS + 640, 128), BF16),
                pltpu.VMEM((NBLK * SLOTS + 640, 128), BF16),
                pltpu.VMEM((8 * TOK, 128), BF16),
                pltpu.VMEM((8 * TOK, 1), F32),
                pltpu.VMEM((8 * TOK, 128), F32),
                pltpu.VMEM((NBLK, 128), jnp.int32),
                pltpu.SMEM((NBLK, 128), jnp.int32),
                pltpu.VMEM((NBLK, 128), jnp.int32),
                pltpu.VMEM((NBLK, 128), jnp.int32),
                pltpu.SemaphoreType.DMA((2,)),
            ],
            compiler_params=pltpu.CompilerParams(vmem_limit_bytes=VMEM_LIMIT),
        )(sink_logits, token_seg, queries, cache_out, own, tseg, pad, gathered)
        projected = pl.pallas_call(
            lambda *refs: project_kernel(nz, *refs),
            name="project",
            out_shape=jax.ShapeDtypeStruct((4 * WCOLS, TOK), BF16),
            in_specs=[VMEM, VMEM, ANY],
            out_specs=VMEM,
            scratch_shapes=[
                pltpu.VMEM((NBLK, WROWS, 128), BF16),
                pltpu.VMEM((nz - 1, WROWS, TOK), BF16),
                pltpu.VMEM((nz - 1, WROWS, TOK), BF16),
                pltpu.SemaphoreType.DMA,
                pltpu.SemaphoreType.DMA((nz - 1,)),
                pltpu.SemaphoreType.DMA((nz - 1,)),
            ],
            compiler_params=pltpu.CompilerParams(
                collective_id=1, has_side_effects=True, vmem_limit_bytes=VMEM_LIMIT
            ),
        )(attention, out_bias.reshape(1, 4 * WCOLS), gathered)
        return projected.T, cache_out.reshape(SLOTS, 1, 128)

    placed = (
        P("gy", "gx"),
        P("gy", "gx", None),
        P("gy", "gx", None),
        P("gy"),
        P("gy"),
        P("gy"),
        P("gy"),
        P("gx"),
        P("gx", "gy"),
        P("gx"),
    )
    return jax.shard_map(
        shards,
        mesh=mesh,
        in_specs=placed,
        out_specs=(P("gy", "gx"), P("gy", "gx", None)),
        check_vma=False,
    )
```

```python
import jax
import jax.numpy as jnp
from jax import lax
from jax.experimental import pallas as pl
from jax.experimental.pallas import tpu as pltpu
from jax.sharding import PartitionSpec as P

MESH = pl.DeviceIdType.MESH
F32 = jnp.float32
BF16 = jnp.bfloat16
NX, NY, NC = 4, 4, 2
NBLK = NX * NY * NC
SLOTS = 512
TOK = 128
META = 16
KVROWS = SLOTS + META
WCOLS = 90
WPAD = 96
WROWS = 4 * WPAD
ROWS = KVROWS + WROWS
PENALTY = -1048576.0
VMEM_LIMIT = 60 * 1024 * 1024
NT = (((1,), (1,)), ((), ()))


def iota(shape, axis):
    return lax.broadcasted_iota(jnp.int32, shape, axis)


def to_column(row):
    return jnp.transpose(jnp.broadcast_to(row, (8, row.shape[1])))[:, :1]


def prep_kernel(new_ref, kv_ref, cseg_ref, cslot_ref, tseg_ref, pad_ref, wt_ref, cache_ref, blk_ref, own_ref):
    own = lax.axis_index("gy")
    target = jnp.where(pad_ref[...] == 1, cslot_ref[...] - own * SLOTS, SLOTS)
    target_f = target.astype(F32)
    tseg_f = tseg_ref[...].astype(F32)
    place = (iota((SLOTS, TOK), 0).astype(F32) == target_f).astype(F32)
    place_b = place.astype(BF16)
    hit_col = jnp.sum(place, axis=1, keepdims=True)
    put = jnp.dot(place_b, new_ref[...], preferred_element_type=F32)
    cache = jnp.where(hit_col > 0.5, put, kv_ref[...].astype(F32)).astype(BF16)
    cache_ref[...] = cache
    order = iota((1, TOK), 1).astype(F32) + 1.0
    which = iota((8, TOK), 0)
    facts = jnp.where(which == 0, tseg_f, jnp.where(which == 1, order, jnp.where(which == 2, 1.0, 0.0)))
    spread = lax.dot_general(facts.astype(BF16), place_b, NT, preferred_element_type=F32)
    hit = spread[2:3] > 0.5
    cseg_f = cseg_ref[...].astype(F32)
    key = jnp.where(hit, spread[0:1], jnp.where(cseg_f < 0.0, 16.0, cseg_f))
    ordered = spread[1:2]
    which = iota((8, SLOTS), 0)
    own_ref[...] = jnp.where(which == 0, key, jnp.where(which == 1, ordered, 0.0))
    double = key * 2.0 + jnp.where(hit, 1.0, 0.0)
    unique = double * SLOTS + iota((1, SLOTS), 1).astype(F32)
    unique_col = to_column(unique)
    rank = jnp.sum((unique_col < unique).astype(F32), axis=0, keepdims=True)
    permute = (iota((SLOTS, SLOTS), 0).astype(F32) == rank).astype(BF16)
    blk_ref[:SLOTS, :] = jnp.dot(permute, cache, preferred_element_type=F32).astype(BF16)
    double_col = to_column(double)
    lane_seg = ((iota((1, 128), 1) - 64) * 2).astype(F32)
    start = jnp.sum((double_col < lane_seg).astype(F32), axis=0, keepdims=True)
    middle = jnp.sum((double_col < lane_seg + 1.0).astype(F32), axis=0, keepdims=True)
    end = jnp.sum((double_col < lane_seg + 2.0).astype(F32), axis=0, keepdims=True)
    rows = []
    for value in (start, middle, end):
        high = jnp.where(value >= 512.0, 2.0, jnp.where(value >= 256.0, 1.0, 0.0))
        rows += [value - 256.0 * high, high]
    which = iota((META, 128), 0)
    meta = jnp.zeros((META, 128), F32)
    for i, row in enumerate(rows):
        meta = jnp.where(which == i, row, meta)
    blk_ref[SLOTS:KVROWS, :] = meta.astype(BF16)
    weights = jnp.concatenate([wt_ref[...].astype(F32), jnp.zeros((WPAD - WCOLS, 4 * 128), F32)], axis=0)
    for k in range(4):
        blk_ref[KVROWS + k * WPAD : KVROWS + (k + 1) * WPAD, :] = weights[:, k * 128 : (k + 1) * 128].astype(BF16)


def splits(rows):
    units = rows // 16
    edges = [0]
    for i in range(4):
        edges.append(edges[-1] + 16 * ((units + 3 - i) // 4))
    return edges


def gather_kernel(copies, blk_ref, out_ref, local_sem, send_sem, recv_sem):
    gx = lax.axis_index("gx")
    gy = lax.axis_index("gy")
    core = gy % NC
    x = (gy // NC) % NX
    y = gy // (NC * NX)

    def index(xx, yy, cc):
        return ((yy % NY) * NX + xx % NX) * NC + cc

    xp, xm = index(x + 1, y, core), index(x + 3, y, core)
    yp, ym = index(x, y + 1, core), index(x, y + 3, core)
    mate = index(x, y, 1 - core)
    barrier = pltpu.get_barrier_semaphore()
    for peer in (xp, xm, yp, ym, mate):
        pl.semaphore_signal(barrier, inc=1, device_id=(gx, peer), device_id_type=MESH)
    own = index(x, y, core)
    local = pltpu.make_async_copy(blk_ref, out_ref.at[own], local_sem)
    local.start()
    pl.semaphore_wait(barrier, 5)
    edges = splits(blk_ref.shape[0])
    used = [0]
    started = []
    mates = []

    def send(block, lo, hi, peer, fresh=False):
        slot = used[0]
        used[0] += 1
        rows = pl.ds(lo, hi - lo)
        source = blk_ref.at[rows] if fresh else out_ref.at[block, rows]
        copy = pltpu.make_async_remote_copy(
            src_ref=source,
            dst_ref=out_ref.at[block, rows],
            send_sem=send_sem.at[slot],
            recv_sem=recv_sem.at[slot],
            device_id=(gx, peer),
            device_id_type=MESH,
        )
        copy.start()
        started.append(copy)
        if peer is mate:
            mates.append(copy)
        return copy

    halves = []
    for half in range(2):
        lo, mid, hi = edges[2 * half], edges[2 * half + 1], edges[2 * half + 2]
        if half == 0:
            first, second = (xp, xm), (yp, ym)
            place = lambda i, j: index(x + i, y + j, core)
        else:
            first, second = (yp, ym), (xp, xm)
            place = lambda i, j: index(x + j, y + i, core)
        halves.append((lo, mid, hi, first, second, place))

    near = []
    for lo, mid, hi, first, second, place in halves:
        a = send(own, lo, hi, first[0], True)
        b = send(own, lo, hi, first[1], True)
        near.append((a, b))
    far = [[] for _ in halves]
    for h, (lo, mid, hi, first, second, place) in enumerate(halves):
        c = send(own, lo, hi, second[0], True)
        d = send(own, lo, hi, second[1], True)
        far[h].append((0, lo, mid, hi, c, d))
        send(own, lo, hi, mate, True)
    forward = []
    for h, (lo, mid, hi, first, second, place) in enumerate(halves):
        a, b = near[h]
        a.wait_recv()
        fa = send(place(3, 0), lo, mid, first[0])
        c = send(place(3, 0), lo, hi, second[0])
        d = send(place(3, 0), lo, hi, second[1])
        far[h].append((3, lo, mid, hi, c, d))
        b.wait_recv()
        fb = send(place(1, 0), mid, hi, first[1])
        c = send(place(1, 0), lo, hi, second[0])
        d = send(place(1, 0), lo, hi, second[1])
        far[h].append((1, lo, mid, hi, c, d))
        send(place(3, 0), lo, hi, mate)
        send(place(1, 0), lo, hi, mate)
        forward.append((fa, fb))
    last = []

    def relay(h, entry):
        i, lo, mid, hi, c, d = entry
        _, _, _, _, second, place = halves[h]
        c.wait_recv()
        last.append(send(place(i, 3), lo, mid, second[0]))
        d.wait_recv()
        last.append(send(place(i, 1), mid, hi, second[1]))
        send(place(i, 3), lo, hi, mate)
        send(place(i, 1), lo, hi, mate)

    for h in range(2):
        relay(h, far[h][0])
    pieces = []
    for h, (lo, mid, hi, first, second, place) in enumerate(halves):
        fa, fb = forward[h]
        fa.wait_recv()
        c0 = send(place(2, 0), lo, mid, second[0])
        d0 = send(place(2, 0), lo, mid, second[1])
        fb.wait_recv()
        c1 = send(place(2, 0), mid, hi, second[0])
        d1 = send(place(2, 0), mid, hi, second[1])
        send(place(2, 0), lo, hi, mate)
        pieces.append((c0, d0, c1, d1))
    for e in range(1, 3):
        for h in range(2):
            relay(h, far[h][e])
    for h, (lo, mid, hi, first, second, place) in enumerate(halves):
        c0, d0, c1, d1 = pieces[h]
        c0.wait_recv()
        last.append(send(place(2, 3), lo, mid, second[0]))
        d1.wait_recv()
        last.append(send(place(2, 1), mid, hi, second[1]))
        c1.wait_recv()
        send(place(2, 3), lo, hi, mate)
        d0.wait_recv()
        send(place(2, 1), lo, hi, mate)
    order = [(0, 0), (1, 0), (0, 3), (1, 3), (0, 1), (1, 1), (0, 2), (1, 2)]
    for n, (h, i) in enumerate(order):
        lo, mid, hi, first, second, place = halves[h]
        last[2 * n].wait_recv()
        last[2 * n + 1].wait_recv()
        send(place(i, 2), lo, hi, mate)
    for copy in mates:
        copy.wait_recv()
    for copy in started:
        copy.wait_send()
    local.wait()
    assert used[0] == copies


def attend_kernel(
    sink_ref, tseg_s, q_ref, cache_ref, own_ref, tseg_ref, pad_ref, g_ref,
    out_ref, buf, ka, va, qa, m_ref, acc_ref, bound_v, bound_s, lo_ref, hi_ref, sems,
):
    own_block = lax.axis_index("gy")
    load = pltpu.make_async_copy(g_ref.at[:, pl.ds(0, KVROWS)], buf.at[:, pl.ds(0, KVROWS)], sems.at[0])
    load.start()
    lane = iota((1, 128), 1)
    low = lane < 64
    tseg_col = to_column(tseg_ref[...].astype(F32))
    pad_col = to_column(pad_ref[...].astype(F32))
    seg_hot = (tseg_col == (lane - 64).astype(F32)).astype(F32)
    for pair in range(4):
        two = q_ref[:, pair * 128 : (pair + 1) * 128].astype(F32) * 0.125
        qa[2 * pair * TOK : (2 * pair + 1) * TOK, :] = jnp.where(low, two, seg_hot).astype(BF16)
        qa[(2 * pair + 1) * TOK : (2 * pair + 2) * TOK, :] = jnp.where(low, pltpu.roll(two, 64, 1), seg_hot).astype(BF16)
    position = iota((TOK, 1), 0).astype(F32) + 1.0
    shown = (own_ref[0:1, :] == tseg_col) & (own_ref[1:2, :] <= position)
    bias = jnp.where(shown, 0.0, PENALTY)
    kv = cache_ref[...].astype(F32)
    k_own = jnp.where(low, kv, 0.0).astype(BF16)
    v_own = jnp.where(low, 1.0, kv).astype(BF16)
    for h in range(8):
        rows = slice(h * TOK, (h + 1) * TOK)
        scores = lax.dot_general(qa[rows, :], k_own, NT, preferred_element_type=F32) + bias
        peak = jnp.maximum(jnp.max(scores, axis=1, keepdims=True), sink_ref[h])
        weights = jnp.exp(scores - peak)
        acc = jnp.dot(weights.astype(BF16), v_own, preferred_element_type=F32)
        acc_ref[rows, :] = acc + jnp.where(low, jnp.exp(sink_ref[h] - peak), 0.0)
        m_ref[rows, :] = peak
    load.wait()
    seg_lo, seg_hi = tseg_s[0], tseg_s[TOK - 1]
    for b in range(NBLK):
        meta = buf[b, SLOTS:KVROWS, :].astype(F32)
        start = meta[0:1] + 256.0 * meta[1:2]
        middle = meta[2:3] + 256.0 * meta[3:4]
        end = meta[4:5] + 256.0 * meta[5:6]
        lo_ref[b : b + 1, :] = start.astype(jnp.int32)
        hi_ref[b : b + 1, :] = jnp.where(b < own_block, end, middle).astype(jnp.int32)
    lo_all, hi_all = lo_ref[...], hi_ref[...]
    wide = iota((NBLK, 128), 1)
    begin = jnp.sum(jnp.where(wide == seg_lo + 64, lo_all, 0).astype(F32), axis=1, keepdims=True)
    stop = jnp.sum(jnp.where(wide == seg_hi + 64, hi_all, 0).astype(F32), axis=1, keepdims=True)
    bound_v[...] = jnp.where(wide == 0, begin, jnp.where(wide == 1, stop, 0.0)).astype(jnp.int32)
    fetch = pltpu.make_async_copy(bound_v, bound_s, sems.at[1])
    fetch.start()
    fetch.wait()

    def pack_block(b, off):
        first, stop = bound_s[b, 0], bound_s[b, 1]
        base = (first // 16) * 16
        length = jnp.where((b == own_block) | (stop <= first), 0, stop - base)
        low_row = lo_ref[pl.ds(b, 1), :]
        high_row = hi_ref[pl.ds(b, 1), :]

        def piece(i, carry):
            src = pl.multiple_of(base + 64 * i, 16)
            dst = pl.multiple_of(off + 64 * i, 16)
            row = src + iota((64, 128), 0)
            kv = jnp.where(row < SLOTS, buf[b, pl.ds(src, 64), :].astype(F32), 0.0)
            penalty = jnp.where((row >= low_row) & (row < high_row), 0.0, PENALTY)
            ka[pl.ds(dst, 64), :] = jnp.where(low, kv, penalty).astype(BF16)
            va[pl.ds(dst, 64), :] = jnp.where(low, 1.0, kv).astype(BF16)
            return carry

        lax.fori_loop(0, (length + 63) // 64, piece, 0)
        return off + ((length + 15) // 16) * 16

    total = lax.fori_loop(0, NBLK, pack_block, 0)
    tail = pl.multiple_of(total, 16)
    ka[pl.ds(tail, 512), :] = jnp.broadcast_to(jnp.where(low, 0.0, PENALTY), (512, 128)).astype(BF16)
    va[pl.ds(tail, 512), :] = jnp.broadcast_to(jnp.where(low, 1.0, 0.0), (512, 128)).astype(BF16)

    def chunk(i, carry):
        at = pl.multiple_of(i * 512, 512)
        keys, values = ka[pl.ds(at, 512), :], va[pl.ds(at, 512), :]
        for r in range(4):
            rows = slice(r * 256, (r + 1) * 256)
            scores = lax.dot_general(qa[rows, :], keys, NT, preferred_element_type=F32)
            old = m_ref[rows, :]
            peak = jnp.maximum(old, jnp.max(scores, axis=1, keepdims=True))
            weights = jnp.exp(scores - peak)
            acc = jnp.dot(weights.astype(BF16), values, preferred_element_type=F32)
            acc_ref[rows, :] = acc_ref[rows, :] * jnp.exp(old - peak) + acc
            m_ref[rows, :] = peak
        return carry

    lax.fori_loop(0, (total + 511) // 512, chunk, 0)
    for pair in range(4):
        even = acc_ref[2 * pair * TOK : (2 * pair + 1) * TOK, :]
        odd = acc_ref[(2 * pair + 1) * TOK : (2 * pair + 2) * TOK, :]
        top = jnp.where(low, pltpu.roll(even, 64, 1), odd)
        bottom = jnp.where(low, even, pltpu.roll(odd, 64, 1))
        out_ref[:, pair * 128 : (pair + 1) * 128] = (top / bottom * pad_col).astype(BF16)


def project_kernel(nz, attn_ref, g_ref, out_ref, wbuf, sbuf, rbuf, load_sem, send_sem, recv_sem):
    gx = lax.axis_index("gx")
    gy = lax.axis_index("gy")
    barrier = pltpu.get_barrier_semaphore()
    for d in (1, nz - 1):
        pl.semaphore_signal(barrier, inc=1, device_id=((gx + d) % nz, gy), device_id_type=MESH)
    far = nz // 2
    offsets = [far]
    for d in range(far - 1, 0, -1):
        offsets += [d, -d]
    offsets.append(0)
    loads = {}
    for n, d in enumerate(offsets):
        blocks = pl.ds(((gx + d + nz) % nz) * 4, 4)
        loads[d] = pltpu.make_async_copy(g_ref.at[blocks, pl.ds(KVROWS, WROWS)], wbuf.at[blocks], load_sem.at[n])
        loads[d].start()

    def partial(d):
        loads[d].wait()
        dest = (gx + d + nz) % nz
        total = None
        for k in (0, 2):
            sides = []
            for kk in (k, k + 1):
                rows = [wbuf[dest * 4 + b, kk * WPAD : (kk + 1) * WPAD, :] for b in range(4)]
                sides.append(jnp.concatenate(rows, axis=0))
            part = lax.dot_general(
                jnp.concatenate(sides, axis=1),
                attn_ref[:, k * 128 : (k + 2) * 128],
                NT,
                preferred_element_type=F32,
            )
            total = part if total is None else total + part
        return total

    def piece(p):
        return slice(p * WPAD, (p + 1) * WPAD)

    copies = {}
    waiting = []

    def flush():
        while waiting:
            side, step, p = waiting.pop(0)
            copy = pltpu.make_async_remote_copy(
                src_ref=sbuf.at[side, step, pl.ds(p * WPAD, WPAD)],
                dst_ref=rbuf.at[side, step, pl.ds(p * WPAD, WPAD)],
                send_sem=send_sem.at[side, step, p],
                recv_sem=recv_sem.at[side, step, p],
                device_id=((gx + (1 if side == 0 else nz - 1)) % nz, gy),
                device_id_type=MESH,
            )
            copy.start()
            copies[side, step, p] = copy

    def put(side, step, p, part):
        value = part[piece(p)]
        earlier = copies.get((side, step - 1, p))
        if earlier is not None:
            earlier.wait_recv()
            value = value + rbuf[side, step - 1, piece(p), :].astype(F32)
        sbuf[side, step, piece(p), :] = value.astype(BF16)
        flush()
        waiting.append((side, step, p))

    first = [(0, 2), (1, 0), (0, 3), (1, 1)]
    second = [(0, 0), (1, 2), (0, 1), (1, 3)]
    part = partial(far)
    for side, p in second:
        sbuf[side, 0, piece(p), :] = part[piece(p)].astype(BF16)
    plus, minus = partial(far - 1), partial(1 - far)
    pl.semaphore_wait(barrier, 2)
    waiting += [(side, 0, p) for side, p in second]
    flush()
    for step in range(1, far):
        for side, p in first:
            put(side, step, p, minus if side else plus)
        if step == 1:
            ahead = partial(far - 2)
            flush()
            ahead = (ahead, partial(2 - far))
        for side, p in second:
            put(side, step, p, minus if side else plus)
        if step > 1:
            d = far - step - 1
            ahead = partial(d)
            flush()
            if d > 0:
                ahead = (ahead, partial(-d))
        else:
            flush()
        if step + 1 < far:
            plus, minus = ahead
    own = ahead
    flush()
    sums = [None] * 4
    for p in (2, 0, 3, 1):
        total = own[piece(p)]
        for side in range(2):
            copies[side, far - 1, p].wait_recv()
            total = total + rbuf[side, far - 1, piece(p), :].astype(F32)
        sums[p] = total[:WCOLS]
    out_ref[...] = jnp.concatenate(sums, axis=0)
    for copy in copies.values():
        copy.wait_send()


VMEM = pl.BlockSpec(memory_space=pltpu.VMEM)
SMEM = pl.BlockSpec(memory_space=pltpu.SMEM)
ANY = pl.BlockSpec(memory_space=pl.ANY)


def solution(mesh):
    nz = mesh.shape["gx"]
    copies = 76

    def shards(queries, new_kv, kv_cache, cache_seg, cache_slot, token_seg, pad_mask, sink_logits, out_weight, out_bias):
        new2 = new_kv.reshape(TOK, 128)
        kv2 = kv_cache.reshape(SLOTS, 128)
        tseg = token_seg.reshape(1, TOK)
        pad = pad_mask.reshape(1, TOK)
        cache_out, block, own = pl.pallas_call(
            prep_kernel,
            name="prep",
            out_shape=(
                jax.ShapeDtypeStruct((SLOTS, 128), BF16),
                jax.ShapeDtypeStruct((ROWS, 128), BF16),
                jax.ShapeDtypeStruct((8, SLOTS), F32),
            ),
            in_specs=[VMEM] * 7,
            out_specs=(VMEM,) * 3,
            compiler_params=pltpu.CompilerParams(vmem_limit_bytes=VMEM_LIMIT),
        )(new2, kv2, cache_seg.reshape(1, SLOTS), cache_slot.reshape(1, TOK), tseg, pad, out_weight.T)
        gathered = pl.pallas_call(
            lambda *refs: gather_kernel(copies, *refs),
            name="gather",
            out_shape=jax.ShapeDtypeStruct((NBLK, ROWS, 128), BF16),
            in_specs=[VMEM],
            out_specs=ANY,
            scratch_shapes=[
                pltpu.SemaphoreType.DMA,
                pltpu.SemaphoreType.DMA((copies,)),
                pltpu.SemaphoreType.DMA((copies,)),
            ],
            compiler_params=pltpu.CompilerParams(collective_id=0, has_side_effects=True),
        )(block)
        attention = pl.pallas_call(
            attend_kernel,
            name="attend",
            out_shape=jax.ShapeDtypeStruct((TOK, 512), BF16),
            in_specs=[SMEM, SMEM, VMEM, VMEM, VMEM, VMEM, VMEM, ANY],
            out_specs=VMEM,
            scratch_shapes=[
                pltpu.VMEM((NBLK, SLOTS + 80, 128), BF16),
                pltpu.VMEM((NBLK * SLOTS + 640, 128), BF16),
                pltpu.VMEM((NBLK * SLOTS + 640, 128), BF16),
                pltpu.VMEM((8 * TOK, 128), BF16),
                pltpu.VMEM((8 * TOK, 1), F32),
                pltpu.VMEM((8 * TOK, 128), F32),
                pltpu.VMEM((NBLK, 128), jnp.int32),
                pltpu.SMEM((NBLK, 128), jnp.int32),
                pltpu.VMEM((NBLK, 128), jnp.int32),
                pltpu.VMEM((NBLK, 128), jnp.int32),
                pltpu.SemaphoreType.DMA((2,)),
            ],
            compiler_params=pltpu.CompilerParams(vmem_limit_bytes=VMEM_LIMIT),
        )(sink_logits, token_seg, queries, cache_out, own, tseg, pad, gathered)
        projected = pl.pallas_call(
            lambda *refs: project_kernel(nz, *refs),
            name="project",
            out_shape=jax.ShapeDtypeStruct((4 * WCOLS, TOK), F32),
            in_specs=[VMEM, ANY],
            out_specs=VMEM,
            scratch_shapes=[
                pltpu.VMEM((NBLK, WROWS, 128), BF16),
                pltpu.VMEM((2, nz // 2, WROWS, TOK), BF16),
                pltpu.VMEM((2, nz // 2, WROWS, TOK), BF16),
                pltpu.SemaphoreType.DMA((nz,)),
                pltpu.SemaphoreType.DMA((2, nz // 2, 4)),
                pltpu.SemaphoreType.DMA((2, nz // 2, 4)),
            ],
            compiler_params=pltpu.CompilerParams(
                collective_id=1, has_side_effects=True, vmem_limit_bytes=VMEM_LIMIT
            ),
        )(attention, gathered)
        attended = (projected.T + out_bias).astype(BF16)
        return attended, cache_out.reshape(SLOTS, 1, 128)

    placed = (
        P("gy", "gx"),
        P("gy", "gx", None),
        P("gy", "gx", None),
        P("gy"),
        P("gy"),
        P("gy"),
        P("gy"),
        P("gx"),
        P("gx", "gy"),
        P("gx"),
    )
    return jax.shard_map(
        shards,
        mesh=mesh,
        in_specs=placed,
        out_specs=(P("gy", "gx"), P("gy", "gx", None)),
        check_vma=False,
    )
```

```python
import jax
import jax.numpy as jnp
from jax import lax
from jax.experimental import pallas as pl
from jax.experimental.pallas import tpu as pltpu
from jax.sharding import PartitionSpec as P

MESH = pl.DeviceIdType.MESH
F32 = jnp.float32
BF16 = jnp.bfloat16
NX, NY, NC = 4, 4, 2
NBLK = NX * NY * NC
SLOTS = 512
TOK = 128
META = 16
KVROWS = SLOTS + META
WCOLS = 90
WPAD = 96
WROWS = 4 * WPAD
LOADS = 4
ROWS = KVROWS + WROWS
PENALTY = -1048576.0
VMEM_LIMIT = 60 * 1024 * 1024
NT = (((1,), (1,)), ((), ()))


def iota(shape, axis):
    return lax.broadcasted_iota(jnp.int32, shape, axis)


def to_column(row):
    return jnp.transpose(jnp.broadcast_to(row, (8, row.shape[1])))[:, :1]


def prep_kernel(new_ref, kv_ref, cseg_ref, cslot_ref, tseg_ref, pad_ref, wt_ref, cache_ref, blk_ref, own_ref):
    own = lax.axis_index("gy")
    target = jnp.where(pad_ref[...] == 1, cslot_ref[...] - own * SLOTS, SLOTS)
    target_f = target.astype(F32)
    tseg_f = tseg_ref[...].astype(F32)
    place = (iota((SLOTS, TOK), 0).astype(F32) == target_f).astype(F32)
    place_b = place.astype(BF16)
    hit_col = jnp.sum(place, axis=1, keepdims=True)
    put = jnp.dot(place_b, new_ref[...], preferred_element_type=F32)
    cache = jnp.where(hit_col > 0.5, put, kv_ref[...].astype(F32)).astype(BF16)
    cache_ref[...] = cache
    order = iota((1, TOK), 1).astype(F32) + 1.0
    which = iota((8, TOK), 0)
    facts = jnp.where(which == 0, tseg_f, jnp.where(which == 1, order, jnp.where(which == 2, 1.0, 0.0)))
    spread = lax.dot_general(facts.astype(BF16), place_b, NT, preferred_element_type=F32)
    hit = spread[2:3] > 0.5
    cseg_f = cseg_ref[...].astype(F32)
    key = jnp.where(hit, spread[0:1], jnp.where(cseg_f < 0.0, 16.0, cseg_f))
    ordered = spread[1:2]
    which = iota((8, SLOTS), 0)
    own_ref[...] = jnp.where(which == 0, key, jnp.where(which == 1, ordered, 0.0))
    double = key * 2.0 + jnp.where(hit, 1.0, 0.0)
    unique = double * SLOTS + iota((1, SLOTS), 1).astype(F32)
    unique_col = to_column(unique)
    rank = jnp.sum((unique_col < unique).astype(F32), axis=0, keepdims=True)
    permute = (iota((SLOTS, SLOTS), 0).astype(F32) == rank).astype(BF16)
    blk_ref[:SLOTS, :] = jnp.dot(permute, cache, preferred_element_type=F32).astype(BF16)
    double_col = to_column(double)
    lane_seg = ((iota((1, 128), 1) - 64) * 2).astype(F32)
    start = jnp.sum((double_col < lane_seg).astype(F32), axis=0, keepdims=True)
    middle = jnp.sum((double_col < lane_seg + 1.0).astype(F32), axis=0, keepdims=True)
    end = jnp.sum((double_col < lane_seg + 2.0).astype(F32), axis=0, keepdims=True)
    rows = []
    for value in (start, middle, end):
        high = jnp.where(value >= 512.0, 2.0, jnp.where(value >= 256.0, 1.0, 0.0))
        rows += [value - 256.0 * high, high]
    which = iota((META, 128), 0)
    meta = jnp.zeros((META, 128), F32)
    for i, row in enumerate(rows):
        meta = jnp.where(which == i, row, meta)
    blk_ref[SLOTS:KVROWS, :] = meta.astype(BF16)
    weights = jnp.concatenate([wt_ref[...].astype(F32), jnp.zeros((WPAD - WCOLS, 4 * 128), F32)], axis=0)
    for k in range(4):
        blk_ref[KVROWS + k * WPAD : KVROWS + (k + 1) * WPAD, :] = weights[:, k * 128 : (k + 1) * 128].astype(BF16)


def splits(rows):
    units = rows // 16
    edges = [0]
    for i in range(4):
        edges.append(edges[-1] + 16 * ((units + 3 - i) // 4))
    return edges


def gather_kernel(
    copies, sink_ref, q_ref, cache_ref, own_ref, tseg_ref, blk_ref,
    out_ref, qa_out, state_out, qa, state, local_sem, save_sem, send_sem, recv_sem,
):
    gx = lax.axis_index("gx")
    gy = lax.axis_index("gy")
    core = gy % NC
    x = (gy // NC) % NX
    y = gy // (NC * NX)

    def index(xx, yy, cc):
        return ((yy % NY) * NX + xx % NX) * NC + cc

    xp, xm = index(x + 1, y, core), index(x + 3, y, core)
    yp, ym = index(x, y + 1, core), index(x, y + 3, core)
    mate = index(x, y, 1 - core)
    barrier = pltpu.get_barrier_semaphore()
    for peer in (xp, xm, yp, ym, mate):
        pl.semaphore_signal(barrier, inc=1, device_id=(gx, peer), device_id_type=MESH)
    own = index(x, y, core)
    local = pltpu.make_async_copy(blk_ref, out_ref.at[own], local_sem)
    local.start()
    pl.semaphore_wait(barrier, 5)
    edges = splits(blk_ref.shape[0])
    used = [0]
    started = []
    mates = []

    def send(block, lo, hi, peer, fresh=False):
        slot = used[0]
        used[0] += 1
        rows = pl.ds(lo, hi - lo)
        source = blk_ref.at[rows] if fresh else out_ref.at[block, rows]
        copy = pltpu.make_async_remote_copy(
            src_ref=source,
            dst_ref=out_ref.at[block, rows],
            send_sem=send_sem.at[slot],
            recv_sem=recv_sem.at[slot],
            device_id=(gx, peer),
            device_id_type=MESH,
        )
        copy.start()
        started.append(copy)
        if peer is mate:
            mates.append(copy)
        return copy

    halves = []
    for half in range(2):
        lo, mid, hi = edges[2 * half], edges[2 * half + 1], edges[2 * half + 2]
        if half == 0:
            first, second = (xp, xm), (yp, ym)
            place = lambda i, j: index(x + i, y + j, core)
        else:
            first, second = (yp, ym), (xp, xm)
            place = lambda i, j: index(x + j, y + i, core)
        halves.append((lo, mid, hi, first, second, place))

    near = []
    for lo, mid, hi, first, second, place in halves:
        a = send(own, lo, hi, first[0], True)
        b = send(own, lo, hi, first[1], True)
        near.append((a, b))
    far = [[] for _ in halves]
    for h, (lo, mid, hi, first, second, place) in enumerate(halves):
        c = send(own, lo, hi, second[0], True)
        d = send(own, lo, hi, second[1], True)
        far[h].append((0, lo, mid, hi, c, d))
        send(own, lo, hi, mate, True)
    lane = iota((1, 128), 1)
    low = lane < 64
    tseg_col = to_column(tseg_ref[...].astype(F32))
    seg_hot = (tseg_col == (lane - 64).astype(F32)).astype(F32)
    shift = (iota((128, 128), 0) == iota((128, 128), 1) + 64).astype(BF16)
    for pair in range(4):
        two = q_ref[:, pair * 128 : (pair + 1) * 128].astype(F32) * 0.125
        odd = jnp.dot(two.astype(BF16), shift, preferred_element_type=F32)
        qa[2 * pair * TOK : (2 * pair + 1) * TOK, :] = jnp.where(low, two, seg_hot).astype(BF16)
        qa[(2 * pair + 1) * TOK : (2 * pair + 2) * TOK, :] = jnp.where(low, odd, seg_hot).astype(BF16)
    position = iota((TOK, 1), 0).astype(F32) + 1.0
    shown = (own_ref[0:1, :] == tseg_col) & (own_ref[1:2, :] <= position)
    bias = jnp.where(shown, 0.0, PENALTY)
    kv = cache_ref[...].astype(F32)
    k_own = jnp.where(low, kv, 0.0).astype(BF16)
    v_own = jnp.where(low, 1.0, kv).astype(BF16)
    for h in range(8):
        rows = slice(h * TOK, (h + 1) * TOK)
        scores = lax.dot_general(qa[rows, :], k_own, NT, preferred_element_type=F32) + bias
        peak = jnp.maximum(jnp.max(scores, axis=1, keepdims=True), sink_ref[h])
        weights = jnp.exp(scores - peak)
        acc = jnp.dot(weights.astype(BF16), v_own, preferred_element_type=F32)
        acc = acc + jnp.where(low, jnp.exp(sink_ref[h] - peak), 0.0)
        state[rows, :] = jnp.where((lane >= 32) & low, peak, acc)
    forward = []
    for h, (lo, mid, hi, first, second, place) in enumerate(halves):
        a, b = near[h]
        a.wait_recv()
        fa = send(place(3, 0), lo, mid, first[0])
        c = send(place(3, 0), lo, hi, second[0])
        d = send(place(3, 0), lo, hi, second[1])
        far[h].append((3, lo, mid, hi, c, d))
        b.wait_recv()
        fb = send(place(1, 0), mid, hi, first[1])
        c = send(place(1, 0), lo, hi, second[0])
        d = send(place(1, 0), lo, hi, second[1])
        far[h].append((1, lo, mid, hi, c, d))
        send(place(3, 0), lo, hi, mate)
        send(place(1, 0), lo, hi, mate)
        forward.append((fa, fb))
    last = []

    def relay(h, entry):
        i, lo, mid, hi, c, d = entry
        _, _, _, _, second, place = halves[h]
        c.wait_recv()
        last.append(send(place(i, 3), lo, mid, second[0]))
        d.wait_recv()
        last.append(send(place(i, 1), mid, hi, second[1]))
        send(place(i, 3), lo, hi, mate)
        send(place(i, 1), lo, hi, mate)

    for h in range(2):
        relay(h, far[h][0])
    saves = [
        pltpu.make_async_copy(qa, qa_out, save_sem.at[0]),
        pltpu.make_async_copy(state, state_out, save_sem.at[1]),
    ]
    for copy in saves:
        copy.start()
    pieces = []
    for h, (lo, mid, hi, first, second, place) in enumerate(halves):
        fa, fb = forward[h]
        fa.wait_recv()
        c0 = send(place(2, 0), lo, mid, second[0])
        d0 = send(place(2, 0), lo, mid, second[1])
        fb.wait_recv()
        c1 = send(place(2, 0), mid, hi, second[0])
        d1 = send(place(2, 0), mid, hi, second[1])
        send(place(2, 0), lo, hi, mate)
        pieces.append((c0, d0, c1, d1))
    for e in range(1, 3):
        for h in range(2):
            relay(h, far[h][e])
    for h, (lo, mid, hi, first, second, place) in enumerate(halves):
        c0, d0, c1, d1 = pieces[h]
        c0.wait_recv()
        last.append(send(place(2, 3), lo, mid, second[0]))
        d1.wait_recv()
        last.append(send(place(2, 1), mid, hi, second[1]))
        c1.wait_recv()
        send(place(2, 3), lo, hi, mate)
        d0.wait_recv()
        send(place(2, 1), lo, hi, mate)
    order = [(0, 0), (1, 0), (0, 3), (1, 3), (0, 1), (1, 1), (0, 2), (1, 2)]
    for n, (h, i) in enumerate(order):
        lo, mid, hi, first, second, place = halves[h]
        last[2 * n].wait_recv()
        last[2 * n + 1].wait_recv()
        send(place(i, 2), lo, hi, mate)
    for copy in mates:
        copy.wait_recv()
    for copy in started:
        copy.wait_send()
    local.wait()
    for copy in saves:
        copy.wait()
    assert used[0] == copies


def attend_kernel(
    tseg_s, pad_ref, qa_in, state_in, g_ref,
    out_ref, buf, heads, ka, va, qa, m_ref, acc_ref, bound_v, bound_s, lo_ref, hi_ref, sems,
):
    own_block = lax.axis_index("gy")
    head = pltpu.make_async_copy(g_ref.at[:, pl.ds(SLOTS, META)], heads, sems.at[0])
    head.start()
    loads = []
    for n in range(LOADS):
        part = pl.ds(n * (NBLK // LOADS), NBLK // LOADS)
        loads.append(
            pltpu.make_async_copy(g_ref.at[part, pl.ds(0, SLOTS)], buf.at[part, pl.ds(0, SLOTS)], sems.at[2 + n])
        )
        loads[-1].start()
    restore = [
        pltpu.make_async_copy(qa_in, qa, sems.at[2 + LOADS]),
        pltpu.make_async_copy(state_in, acc_ref, sems.at[3 + LOADS]),
    ]
    for copy in restore:
        copy.start()
    lane = iota((1, 128), 1)
    low = lane < 64
    pad_col = to_column(pad_ref[...].astype(F32))
    head.wait()
    seg_lo, seg_hi = tseg_s[0], tseg_s[TOK - 1]
    for b in range(NBLK):
        meta = heads[b].astype(F32)
        start = meta[0:1] + 256.0 * meta[1:2]
        middle = meta[2:3] + 256.0 * meta[3:4]
        end = meta[4:5] + 256.0 * meta[5:6]
        lo_ref[b : b + 1, :] = start.astype(jnp.int32)
        hi_ref[b : b + 1, :] = jnp.where(b < own_block, end, middle).astype(jnp.int32)
    lo_all, hi_all = lo_ref[...], hi_ref[...]
    wide = iota((NBLK, 128), 1)
    begin = jnp.sum(jnp.where(wide == seg_lo + 64, lo_all, 0).astype(F32), axis=1, keepdims=True)
    stop = jnp.sum(jnp.where(wide == seg_hi + 64, hi_all, 0).astype(F32), axis=1, keepdims=True)
    bound_v[...] = jnp.where(wide == 0, begin, jnp.where(wide == 1, stop, 0.0)).astype(jnp.int32)
    fetch = pltpu.make_async_copy(bound_v, bound_s, sems.at[1])
    fetch.start()
    fetch.wait()

    def pack_block(b, off):
        first, stop = bound_s[b, 0], bound_s[b, 1]
        base = (first // 16) * 16
        length = jnp.where((b == own_block) | (stop <= first), 0, stop - base)
        low_row = lo_ref[pl.ds(b, 1), :]
        high_row = hi_ref[pl.ds(b, 1), :]

        def piece(i, carry):
            src = pl.multiple_of(base + 64 * i, 16)
            dst = pl.multiple_of(off + 64 * i, 16)
            row = src + iota((64, 128), 0)
            kv = jnp.where(row < SLOTS, buf[b, pl.ds(src, 64), :].astype(F32), 0.0)
            penalty = jnp.where((row >= low_row) & (row < high_row), 0.0, PENALTY)
            ka[pl.ds(dst, 64), :] = jnp.where(low, kv, penalty).astype(BF16)
            va[pl.ds(dst, 64), :] = jnp.where(low, 1.0, kv).astype(BF16)
            return carry

        lax.fori_loop(0, (length + 63) // 64, piece, 0)
        return off + ((length + 15) // 16) * 16

    total = 0
    for n, load in enumerate(loads):
        load.wait()
        total = lax.fori_loop(n * (NBLK // LOADS), (n + 1) * (NBLK // LOADS), pack_block, total)
    for copy in restore:
        copy.wait()
    m_ref[...] = acc_ref[:, 32:33]
    acc_ref[...] = jnp.where((lane >= 32) & low, pltpu.roll(acc_ref[...], 32, 1), acc_ref[...])
    tail = pl.multiple_of(total, 16)
    ka[pl.ds(tail, 512), :] = jnp.broadcast_to(jnp.where(low, 0.0, PENALTY), (512, 128)).astype(BF16)
    va[pl.ds(tail, 512), :] = jnp.broadcast_to(jnp.where(low, 1.0, 0.0), (512, 128)).astype(BF16)

    def chunk(i, carry):
        at = pl.multiple_of(i * 512, 512)
        keys, values = ka[pl.ds(at, 512), :], va[pl.ds(at, 512), :]
        for r in range(4):
            rows = slice(r * 256, (r + 1) * 256)
            scores = lax.dot_general(qa[rows, :], keys, NT, preferred_element_type=F32)
            old = m_ref[rows, :]
            peak = jnp.maximum(old, jnp.max(scores, axis=1, keepdims=True))
            weights = jnp.exp(scores - peak)
            acc = jnp.dot(weights.astype(BF16), values, preferred_element_type=F32)
            acc_ref[rows, :] = acc_ref[rows, :] * jnp.exp(old - peak) + acc
            m_ref[rows, :] = peak
        return carry

    lax.fori_loop(0, (total + 511) // 512, chunk, 0)
    for pair in range(4):
        even = acc_ref[2 * pair * TOK : (2 * pair + 1) * TOK, :]
        odd = acc_ref[(2 * pair + 1) * TOK : (2 * pair + 2) * TOK, :]
        top = jnp.where(low, pltpu.roll(even, 64, 1), odd)
        bottom = jnp.where(low, even, pltpu.roll(odd, 64, 1))
        out_ref[:, pair * 128 : (pair + 1) * 128] = (top / bottom * pad_col).astype(BF16)


def project_kernel(nz, attn_ref, g_ref, out_ref, wbuf, sbuf, rbuf, load_sem, send_sem, recv_sem):
    gx = lax.axis_index("gx")
    gy = lax.axis_index("gy")
    barrier = pltpu.get_barrier_semaphore()
    for d in (1, nz - 1):
        pl.semaphore_signal(barrier, inc=1, device_id=((gx + d) % nz, gy), device_id_type=MESH)
    far = nz // 2
    offsets = [far]
    for d in range(far - 1, 0, -1):
        offsets += [d, -d]
    offsets.append(0)
    loads = {}
    for n, d in enumerate(offsets):
        blocks = pl.ds(((gx + d + nz) % nz) * 4, 4)
        loads[d] = pltpu.make_async_copy(g_ref.at[blocks, pl.ds(KVROWS, WROWS)], wbuf.at[blocks], load_sem.at[n])
        loads[d].start()

    def partial(d):
        loads[d].wait()
        dest = (gx + d + nz) % nz
        total = None
        for k in (0, 2):
            sides = []
            for kk in (k, k + 1):
                rows = [wbuf[dest * 4 + b, kk * WPAD : (kk + 1) * WPAD, :] for b in range(4)]
                sides.append(jnp.concatenate(rows, axis=0))
            part = lax.dot_general(
                jnp.concatenate(sides, axis=1),
                attn_ref[:, k * 128 : (k + 2) * 128],
                NT,
                preferred_element_type=F32,
            )
            total = part if total is None else total + part
        return total

    def piece(p):
        return slice(p * WPAD, (p + 1) * WPAD)

    copies = {}
    waiting = []

    def flush():
        while waiting:
            side, step, p = waiting.pop(0)
            copy = pltpu.make_async_remote_copy(
                src_ref=sbuf.at[side, step, pl.ds(p * WPAD, WPAD)],
                dst_ref=rbuf.at[side, step, pl.ds(p * WPAD, WPAD)],
                send_sem=send_sem.at[side, step, p],
                recv_sem=recv_sem.at[side, step, p],
                device_id=((gx + (1 if side == 0 else nz - 1)) % nz, gy),
                device_id_type=MESH,
            )
            copy.start()
            copies[side, step, p] = copy

    def put(side, step, p, part):
        value = part[piece(p)]
        earlier = copies.get((side, step - 1, p))
        if earlier is not None:
            earlier.wait_recv()
            value = value + rbuf[side, step - 1, piece(p), :].astype(F32)
        sbuf[side, step, piece(p), :] = value.astype(BF16)
        flush()
        waiting.append((side, step, p))

    first = [(0, 2), (1, 0), (0, 3), (1, 1)]
    second = [(0, 0), (1, 2), (0, 1), (1, 3)]
    part = partial(far)
    for side, p in second:
        sbuf[side, 0, piece(p), :] = part[piece(p)].astype(BF16)
    plus, minus = partial(far - 1), partial(1 - far)
    pl.semaphore_wait(barrier, 2)
    waiting += [(side, 0, p) for side, p in second]
    flush()
    for step in range(1, far):
        for side, p in first:
            put(side, step, p, minus if side else plus)
        if step == 1:
            ahead = partial(far - 2)
            flush()
            ahead = (ahead, partial(2 - far))
        for side, p in second:
            put(side, step, p, minus if side else plus)
        if step > 1:
            d = far - step - 1
            ahead = partial(d)
            flush()
            if d > 0:
                ahead = (ahead, partial(-d))
        else:
            flush()
        if step + 1 < far:
            plus, minus = ahead
    own = ahead
    flush()
    sums = [None] * 4
    for p in (2, 0, 3, 1):
        total = own[piece(p)]
        for side in range(2):
            copies[side, far - 1, p].wait_recv()
            total = total + rbuf[side, far - 1, piece(p), :].astype(F32)
        sums[p] = total[:WCOLS]
    out_ref[...] = jnp.concatenate(sums, axis=0)
    for copy in copies.values():
        copy.wait_send()


VMEM = pl.BlockSpec(memory_space=pltpu.VMEM)
SMEM = pl.BlockSpec(memory_space=pltpu.SMEM)
ANY = pl.BlockSpec(memory_space=pl.ANY)


def solution(mesh):
    nz = mesh.shape["gx"]
    copies = 76

    def shards(queries, new_kv, kv_cache, cache_seg, cache_slot, token_seg, pad_mask, sink_logits, out_weight, out_bias):
        new2 = new_kv.reshape(TOK, 128)
        kv2 = kv_cache.reshape(SLOTS, 128)
        tseg = token_seg.reshape(1, TOK)
        pad = pad_mask.reshape(1, TOK)
        cache_out, block, own = pl.pallas_call(
            prep_kernel,
            name="prep",
            out_shape=(
                jax.ShapeDtypeStruct((SLOTS, 128), BF16),
                jax.ShapeDtypeStruct((ROWS, 128), BF16),
                jax.ShapeDtypeStruct((8, SLOTS), F32),
            ),
            in_specs=[VMEM] * 7,
            out_specs=(VMEM,) * 3,
            compiler_params=pltpu.CompilerParams(vmem_limit_bytes=VMEM_LIMIT),
        )(new2, kv2, cache_seg.reshape(1, SLOTS), cache_slot.reshape(1, TOK), tseg, pad, out_weight.T)
        gathered, qa, state = pl.pallas_call(
            lambda *refs: gather_kernel(copies, *refs),
            name="gather",
            out_shape=(
                jax.ShapeDtypeStruct((NBLK, ROWS, 128), BF16),
                jax.ShapeDtypeStruct((8 * TOK, 128), BF16),
                jax.ShapeDtypeStruct((8 * TOK, 128), F32),
            ),
            in_specs=[SMEM, VMEM, VMEM, VMEM, VMEM, VMEM],
            out_specs=(ANY,) * 3,
            scratch_shapes=[
                pltpu.VMEM((8 * TOK, 128), BF16),
                pltpu.VMEM((8 * TOK, 128), F32),
                pltpu.SemaphoreType.DMA,
                pltpu.SemaphoreType.DMA((2,)),
                pltpu.SemaphoreType.DMA((copies,)),
                pltpu.SemaphoreType.DMA((copies,)),
            ],
            compiler_params=pltpu.CompilerParams(
                collective_id=0, has_side_effects=True, vmem_limit_bytes=VMEM_LIMIT
            ),
        )(sink_logits, queries, cache_out, own, tseg, block)
        attention = pl.pallas_call(
            attend_kernel,
            name="attend",
            out_shape=jax.ShapeDtypeStruct((TOK, 512), BF16),
            in_specs=[SMEM, VMEM, ANY, ANY, ANY],
            out_specs=VMEM,
            scratch_shapes=[
                pltpu.VMEM((NBLK, SLOTS + 80, 128), BF16),
                pltpu.VMEM((NBLK, META, 128), BF16),
                pltpu.VMEM((NBLK * SLOTS + 640, 128), BF16),
                pltpu.VMEM((NBLK * SLOTS + 640, 128), BF16),
                pltpu.VMEM((8 * TOK, 128), BF16),
                pltpu.VMEM((8 * TOK, 1), F32),
                pltpu.VMEM((8 * TOK, 128), F32),
                pltpu.VMEM((NBLK, 128), jnp.int32),
                pltpu.SMEM((NBLK, 128), jnp.int32),
                pltpu.VMEM((NBLK, 128), jnp.int32),
                pltpu.VMEM((NBLK, 128), jnp.int32),
                pltpu.SemaphoreType.DMA((4 + LOADS,)),
            ],
            compiler_params=pltpu.CompilerParams(vmem_limit_bytes=VMEM_LIMIT),
        )(token_seg, pad, qa, state, gathered)
        projected = pl.pallas_call(
            lambda *refs: project_kernel(nz, *refs),
            name="project",
            out_shape=jax.ShapeDtypeStruct((4 * WCOLS, TOK), F32),
            in_specs=[VMEM, ANY],
            out_specs=VMEM,
            scratch_shapes=[
                pltpu.VMEM((NBLK, WROWS, 128), BF16),
                pltpu.VMEM((2, nz // 2, WROWS, TOK), BF16),
                pltpu.VMEM((2, nz // 2, WROWS, TOK), BF16),
                pltpu.SemaphoreType.DMA((nz,)),
                pltpu.SemaphoreType.DMA((2, nz // 2, 4)),
                pltpu.SemaphoreType.DMA((2, nz // 2, 4)),
            ],
            compiler_params=pltpu.CompilerParams(
                collective_id=1, has_side_effects=True, vmem_limit_bytes=VMEM_LIMIT
            ),
        )(attention, gathered)
        attended = (projected.T + out_bias).astype(BF16)
        return attended, cache_out.reshape(SLOTS, 1, 128)

    placed = (
        P("gy", "gx"),
        P("gy", "gx", None),
        P("gy", "gx", None),
        P("gy"),
        P("gy"),
        P("gy"),
        P("gy"),
        P("gx"),
        P("gx", "gy"),
        P("gx"),
    )
    return jax.shard_map(
        shards,
        mesh=mesh,
        in_specs=placed,
        out_specs=(P("gy", "gx"), P("gy", "gx", None)),
        check_vma=False,
    )
```

```python
import jax
import jax.numpy as jnp
from jax import lax
from jax.experimental import pallas as pl
from jax.experimental.pallas import tpu as pltpu
from jax.sharding import PartitionSpec as P

MESH = pl.DeviceIdType.MESH
F32 = jnp.float32
BF16 = jnp.bfloat16
NX, NY, NC = 4, 4, 2
NBLK = NX * NY * NC
SLOTS = 512
TOK = 128
META = 16
KVROWS = SLOTS + META
WCOLS = 90
WPAD = 96
WROWS = 4 * WPAD
LOADS = 4
GROUP = 128
CHUNK = 256
ROWS = KVROWS + WROWS
PENALTY = -1048576.0
VMEM_LIMIT = 60 * 1024 * 1024
NT = (((1,), (1,)), ((), ()))


def iota(shape, axis):
    return lax.broadcasted_iota(jnp.int32, shape, axis)


def to_column(row):
    return jnp.transpose(jnp.broadcast_to(row, (8, row.shape[1])))[:, :1]


def prep_kernel(new_ref, kv_ref, cseg_ref, cslot_ref, tseg_ref, pad_ref, wt_ref, cache_ref, blk_ref, own_ref):
    own = lax.axis_index("gy")
    target = jnp.where(pad_ref[...] == 1, cslot_ref[...] - own * SLOTS, SLOTS)
    target_f = target.astype(F32)
    tseg_f = tseg_ref[...].astype(F32)
    place = (iota((SLOTS, TOK), 0).astype(F32) == target_f).astype(F32)
    place_b = place.astype(BF16)
    hit_col = jnp.sum(place, axis=1, keepdims=True)
    put = jnp.dot(place_b, new_ref[...], preferred_element_type=F32)
    cache = jnp.where(hit_col > 0.5, put, kv_ref[...].astype(F32)).astype(BF16)
    cache_ref[...] = cache
    order = iota((1, TOK), 1).astype(F32) + 1.0
    which = iota((8, TOK), 0)
    facts = jnp.where(which == 0, tseg_f, jnp.where(which == 1, order, jnp.where(which == 2, 1.0, 0.0)))
    spread = lax.dot_general(facts.astype(BF16), place_b, NT, preferred_element_type=F32)
    hit = spread[2:3] > 0.5
    cseg_f = cseg_ref[...].astype(F32)
    key = jnp.where(hit, spread[0:1], jnp.where(cseg_f < 0.0, 16.0, cseg_f))
    ordered = spread[1:2]
    which = iota((8, SLOTS), 0)
    own_ref[...] = jnp.where(which == 0, key, jnp.where(which == 1, ordered, 0.0))
    double = key * 2.0 + jnp.where(hit, 1.0, 0.0)
    unique = double * SLOTS + iota((1, SLOTS), 1).astype(F32)
    unique_col = to_column(unique)
    rank = jnp.sum((unique_col < unique).astype(F32), axis=0, keepdims=True)
    permute = (iota((SLOTS, SLOTS), 0).astype(F32) == rank).astype(BF16)
    blk_ref[:SLOTS, :] = jnp.dot(permute, cache, preferred_element_type=F32).astype(BF16)
    double_col = to_column(double)
    lane_seg = ((iota((1, 128), 1) - 64) * 2).astype(F32)
    start = jnp.sum((double_col < lane_seg).astype(F32), axis=0, keepdims=True)
    middle = jnp.sum((double_col < lane_seg + 1.0).astype(F32), axis=0, keepdims=True)
    end = jnp.sum((double_col < lane_seg + 2.0).astype(F32), axis=0, keepdims=True)
    rows = []
    for value in (start, middle, end):
        high = jnp.where(value >= 512.0, 2.0, jnp.where(value >= 256.0, 1.0, 0.0))
        rows += [value - 256.0 * high, high]
    which = iota((META, 128), 0)
    meta = jnp.zeros((META, 128), F32)
    for i, row in enumerate(rows):
        meta = jnp.where(which == i, row, meta)
    blk_ref[SLOTS:KVROWS, :] = meta.astype(BF16)
    weights = jnp.concatenate([wt_ref[...].astype(F32), jnp.zeros((WPAD - WCOLS, 4 * 128), F32)], axis=0)
    for k in range(4):
        blk_ref[KVROWS + k * WPAD : KVROWS + (k + 1) * WPAD, :] = weights[:, k * 128 : (k + 1) * 128].astype(BF16)


def splits(rows):
    units = rows // 16
    edges = [0]
    for i in range(4):
        edges.append(edges[-1] + 16 * ((units + 3 - i) // 4))
    return edges


def gather_kernel(
    copies, sink_ref, q_ref, cache_ref, own_ref, tseg_ref, blk_ref,
    out_ref, qa_out, state_out, qa, state, local_sem, save_sem, send_sem, recv_sem,
):
    gx = lax.axis_index("gx")
    gy = lax.axis_index("gy")
    core = gy % NC
    x = (gy // NC) % NX
    y = gy // (NC * NX)

    def index(xx, yy, cc):
        return ((yy % NY) * NX + xx % NX) * NC + cc

    xp, xm = index(x + 1, y, core), index(x + 3, y, core)
    yp, ym = index(x, y + 1, core), index(x, y + 3, core)
    mate = index(x, y, 1 - core)
    barrier = pltpu.get_barrier_semaphore()
    for peer in (xp, xm, yp, ym, mate):
        pl.semaphore_signal(barrier, inc=1, device_id=(gx, peer), device_id_type=MESH)
    own = index(x, y, core)
    local = pltpu.make_async_copy(blk_ref, out_ref.at[own], local_sem)
    local.start()
    pl.semaphore_wait(barrier, 5)
    edges = splits(blk_ref.shape[0])
    used = [0]
    started = []
    mates = []

    def send(block, lo, hi, peer, fresh=False):
        slot = used[0]
        used[0] += 1
        rows = pl.ds(lo, hi - lo)
        source = blk_ref.at[rows] if fresh else out_ref.at[block, rows]
        copy = pltpu.make_async_remote_copy(
            src_ref=source,
            dst_ref=out_ref.at[block, rows],
            send_sem=send_sem.at[slot],
            recv_sem=recv_sem.at[slot],
            device_id=(gx, peer),
            device_id_type=MESH,
        )
        copy.start()
        started.append(copy)
        if peer is mate:
            mates.append(copy)
        return copy

    halves = []
    for half in range(2):
        lo, mid, hi = edges[2 * half], edges[2 * half + 1], edges[2 * half + 2]
        if half == 0:
            first, second = (xp, xm), (yp, ym)
            place = lambda i, j: index(x + i, y + j, core)
        else:
            first, second = (yp, ym), (xp, xm)
            place = lambda i, j: index(x + j, y + i, core)
        halves.append((lo, mid, hi, first, second, place))

    near = []
    for lo, mid, hi, first, second, place in halves:
        a = send(own, lo, hi, first[0], True)
        b = send(own, lo, hi, first[1], True)
        near.append((a, b))
    far = [[] for _ in halves]
    for h, (lo, mid, hi, first, second, place) in enumerate(halves):
        c = send(own, lo, hi, second[0], True)
        d = send(own, lo, hi, second[1], True)
        far[h].append((0, lo, mid, hi, c, d))
        send(own, lo, hi, mate, True)
    lane = iota((1, 128), 1)
    low = lane < 64
    tseg_col = to_column(tseg_ref[...].astype(F32))
    seg_hot = (tseg_col == (lane - 64).astype(F32)).astype(F32)
    shift = (iota((128, 128), 0) == iota((128, 128), 1) + 64).astype(BF16)
    for pair in range(4):
        two = q_ref[:, pair * 128 : (pair + 1) * 128].astype(F32) * 0.125
        odd = jnp.dot(two.astype(BF16), shift, preferred_element_type=F32)
        qa[2 * pair * TOK : (2 * pair + 1) * TOK, :] = jnp.where(low, two, seg_hot).astype(BF16)
        qa[(2 * pair + 1) * TOK : (2 * pair + 2) * TOK, :] = jnp.where(low, odd, seg_hot).astype(BF16)
    position = iota((TOK, 1), 0).astype(F32) + 1.0
    shown = (own_ref[0:1, :] == tseg_col) & (own_ref[1:2, :] <= position)
    bias = jnp.where(shown, 0.0, PENALTY)
    kv = cache_ref[...].astype(F32)
    k_own = jnp.where(low, kv, 0.0).astype(BF16)
    v_own = jnp.where(low, 1.0, kv).astype(BF16)
    for h in range(8):
        rows = slice(h * TOK, (h + 1) * TOK)
        scores = lax.dot_general(qa[rows, :], k_own, NT, preferred_element_type=F32) + bias
        peak = jnp.maximum(jnp.max(scores, axis=1, keepdims=True), sink_ref[h])
        weights = jnp.exp(scores - peak)
        acc = jnp.dot(weights.astype(BF16), v_own, preferred_element_type=F32)
        acc = acc + jnp.where(low, jnp.exp(sink_ref[h] - peak), 0.0)
        state[rows, :] = jnp.where((lane >= 32) & low, peak, acc)
    forward = []
    for h, (lo, mid, hi, first, second, place) in enumerate(halves):
        a, b = near[h]
        a.wait_recv()
        fa = send(place(3, 0), lo, mid, first[0])
        c = send(place(3, 0), lo, hi, second[0])
        d = send(place(3, 0), lo, hi, second[1])
        far[h].append((3, lo, mid, hi, c, d))
        b.wait_recv()
        fb = send(place(1, 0), mid, hi, first[1])
        c = send(place(1, 0), lo, hi, second[0])
        d = send(place(1, 0), lo, hi, second[1])
        far[h].append((1, lo, mid, hi, c, d))
        send(place(3, 0), lo, hi, mate)
        send(place(1, 0), lo, hi, mate)
        forward.append((fa, fb))
    last = []

    def relay(h, entry):
        i, lo, mid, hi, c, d = entry
        _, _, _, _, second, place = halves[h]
        c.wait_recv()
        last.append(send(place(i, 3), lo, mid, second[0]))
        d.wait_recv()
        last.append(send(place(i, 1), mid, hi, second[1]))
        send(place(i, 3), lo, hi, mate)
        send(place(i, 1), lo, hi, mate)

    for h in range(2):
        relay(h, far[h][0])
    saves = [
        pltpu.make_async_copy(qa, qa_out, save_sem.at[0]),
        pltpu.make_async_copy(state, state_out, save_sem.at[1]),
    ]
    for copy in saves:
        copy.start()
    pieces = []
    for h, (lo, mid, hi, first, second, place) in enumerate(halves):
        fa, fb = forward[h]
        fa.wait_recv()
        c0 = send(place(2, 0), lo, mid, second[0])
        d0 = send(place(2, 0), lo, mid, second[1])
        fb.wait_recv()
        c1 = send(place(2, 0), mid, hi, second[0])
        d1 = send(place(2, 0), mid, hi, second[1])
        send(place(2, 0), lo, hi, mate)
        pieces.append((c0, d0, c1, d1))
    for e in range(1, 3):
        for h in range(2):
            relay(h, far[h][e])
    for h, (lo, mid, hi, first, second, place) in enumerate(halves):
        c0, d0, c1, d1 = pieces[h]
        c0.wait_recv()
        last.append(send(place(2, 3), lo, mid, second[0]))
        d1.wait_recv()
        last.append(send(place(2, 1), mid, hi, second[1]))
        c1.wait_recv()
        send(place(2, 3), lo, hi, mate)
        d0.wait_recv()
        send(place(2, 1), lo, hi, mate)
    order = [(0, 0), (1, 0), (0, 3), (1, 3), (0, 1), (1, 1), (0, 2), (1, 2)]
    for n, (h, i) in enumerate(order):
        lo, mid, hi, first, second, place = halves[h]
        last[2 * n].wait_recv()
        last[2 * n + 1].wait_recv()
        send(place(i, 2), lo, hi, mate)
    for copy in mates:
        copy.wait_recv()
    for copy in started:
        copy.wait_send()
    local.wait()
    for copy in saves:
        copy.wait()
    assert used[0] == copies


def attend_kernel(
    tseg_s, pad_ref, qa_in, state_in, g_ref,
    out_ref, buf, heads, ka, va, qa, m_ref, acc_ref, bound_v, bound_s, lo_ref, hi_ref, sems,
):
    own_block = lax.axis_index("gy")
    head = pltpu.make_async_copy(g_ref.at[:, pl.ds(SLOTS, META)], heads, sems.at[0])
    head.start()
    loads = []
    for n in range(LOADS):
        part = pl.ds(n * (NBLK // LOADS), NBLK // LOADS)
        loads.append(
            pltpu.make_async_copy(g_ref.at[part, pl.ds(0, SLOTS)], buf.at[part, pl.ds(0, SLOTS)], sems.at[2 + n])
        )
        loads[-1].start()
    restore = [
        pltpu.make_async_copy(qa_in, qa, sems.at[2 + LOADS]),
        pltpu.make_async_copy(state_in, acc_ref, sems.at[3 + LOADS]),
    ]
    for copy in restore:
        copy.start()
    lane = iota((1, 128), 1)
    low = lane < 64
    pad_col = to_column(pad_ref[...].astype(F32))
    head.wait()
    seg_lo, seg_hi = tseg_s[0], tseg_s[TOK - 1]
    for b in range(NBLK):
        meta = heads[b].astype(F32)
        start = meta[0:1] + 256.0 * meta[1:2]
        middle = meta[2:3] + 256.0 * meta[3:4]
        end = meta[4:5] + 256.0 * meta[5:6]
        lo_ref[b : b + 1, :] = start.astype(jnp.int32)
        hi_ref[b : b + 1, :] = jnp.where(b < own_block, end, middle).astype(jnp.int32)
    lo_all, hi_all = lo_ref[...], hi_ref[...]
    wide = iota((NBLK, 128), 1)
    begin = jnp.sum(jnp.where(wide == seg_lo + 64, lo_all, 0).astype(F32), axis=1, keepdims=True)
    stop = jnp.sum(jnp.where(wide == seg_hi + 64, hi_all, 0).astype(F32), axis=1, keepdims=True)
    bound_v[...] = jnp.where(wide == 0, begin, jnp.where(wide == 1, stop, 0.0)).astype(jnp.int32)
    fetch = pltpu.make_async_copy(bound_v, bound_s, sems.at[1])
    fetch.start()
    fetch.wait()

    def pack_block(b, off):
        first, stop = bound_s[b, 0], bound_s[b, 1]
        base = (first // 16) * 16
        length = jnp.where((b == own_block) | (stop <= first), 0, stop - base)
        low_row = lo_ref[pl.ds(b, 1), :]
        high_row = hi_ref[pl.ds(b, 1), :]

        def piece(i, carry):
            src = pl.multiple_of(base + 64 * i, 16)
            dst = pl.multiple_of(off + 64 * i, 16)
            row = src + iota((64, 128), 0)
            kv = jnp.where(row < SLOTS, buf[b, pl.ds(src, 64), :].astype(F32), 0.0)
            penalty = jnp.where((row >= low_row) & (row < high_row), 0.0, PENALTY)
            ka[pl.ds(dst, 64), :] = jnp.where(low, kv, penalty).astype(BF16)
            va[pl.ds(dst, 64), :] = jnp.where(low, 1.0, kv).astype(BF16)
            return carry

        lax.fori_loop(0, (length + 63) // 64, piece, 0)
        return off + ((length + 15) // 16) * 16

    total = 0
    for n, load in enumerate(loads):
        load.wait()
        total = lax.fori_loop(n * (NBLK // LOADS), (n + 1) * (NBLK // LOADS), pack_block, total)
    for copy in restore:
        copy.wait()
    m_ref[...] = jnp.broadcast_to(acc_ref[:, 32:33], (8 * TOK, 128))
    acc_ref[...] = jnp.where((lane >= 32) & low, pltpu.roll(acc_ref[...], 32, 1), acc_ref[...])
    tail = pl.multiple_of(total, 16)
    ka[pl.ds(tail, CHUNK), :] = jnp.broadcast_to(jnp.where(low, 0.0, PENALTY), (CHUNK, 128)).astype(BF16)
    va[pl.ds(tail, CHUNK), :] = jnp.broadcast_to(jnp.where(low, 1.0, 0.0), (CHUNK, 128)).astype(BF16)

    def chunk(i, carry):
        at = pl.multiple_of(i * CHUNK, CHUNK)
        keys, values = ka[pl.ds(at, CHUNK), :], va[pl.ds(at, CHUNK), :]

        def score(r):
            return lax.dot_general(qa[r * GROUP : (r + 1) * GROUP, :], keys, NT, preferred_element_type=F32)

        upcoming = score(0)
        for r in range(8 * TOK // GROUP):
            rows = slice(r * GROUP, (r + 1) * GROUP)
            scores = upcoming
            if (r + 1) * GROUP < 8 * TOK:
                upcoming = score(r + 1)
            old = m_ref[rows, :]
            peak = jnp.maximum(old, jnp.max(scores, axis=1, keepdims=True))
            weights = [jnp.exp(scores[:, c : c + 128] - peak).astype(BF16) for c in range(0, CHUNK, 128)]
            acc = jnp.dot(jnp.concatenate(weights, axis=1), values, preferred_element_type=F32)
            acc_ref[rows, :] = acc_ref[rows, :] * jnp.exp(old - peak) + acc
            m_ref[rows, :] = peak
        return carry

    lax.fori_loop(0, (total + CHUNK - 1) // CHUNK, chunk, 0)
    for pair in range(4):
        even = acc_ref[2 * pair * TOK : (2 * pair + 1) * TOK, :]
        odd = acc_ref[(2 * pair + 1) * TOK : (2 * pair + 2) * TOK, :]
        top = jnp.where(low, pltpu.roll(even, 64, 1), odd)
        bottom = jnp.where(low, even, pltpu.roll(odd, 64, 1))
        out_ref[:, pair * 128 : (pair + 1) * 128] = (top / bottom * pad_col).astype(BF16)


def project_kernel(nz, attn_ref, g_ref, out_ref, wbuf, sbuf, rbuf, load_sem, send_sem, recv_sem):
    gx = lax.axis_index("gx")
    gy = lax.axis_index("gy")
    barrier = pltpu.get_barrier_semaphore()
    for d in (1, nz - 1):
        pl.semaphore_signal(barrier, inc=1, device_id=((gx + d) % nz, gy), device_id_type=MESH)
    far = nz // 2
    offsets = [far]
    for d in range(far - 1, 0, -1):
        offsets += [d, -d]
    offsets.append(0)
    loads = {}
    for n, d in enumerate(offsets):
        blocks = pl.ds(((gx + d + nz) % nz) * 4, 4)
        loads[d] = pltpu.make_async_copy(g_ref.at[blocks, pl.ds(KVROWS, WROWS)], wbuf.at[blocks], load_sem.at[n])
        loads[d].start()

    def partial(d):
        loads[d].wait()
        dest = (gx + d + nz) % nz
        total = None
        for k in (0, 2):
            sides = []
            for kk in (k, k + 1):
                rows = [wbuf[dest * 4 + b, kk * WPAD : (kk + 1) * WPAD, :] for b in range(4)]
                sides.append(jnp.concatenate(rows, axis=0))
            part = lax.dot_general(
                jnp.concatenate(sides, axis=1),
                attn_ref[:, k * 128 : (k + 2) * 128],
                NT,
                preferred_element_type=F32,
            )
            total = part if total is None else total + part
        return total

    def piece(p):
        return slice(p * WPAD, (p + 1) * WPAD)

    copies = {}
    waiting = []

    def flush():
        while waiting:
            side, step, p = waiting.pop(0)
            copy = pltpu.make_async_remote_copy(
                src_ref=sbuf.at[side, step, pl.ds(p * WPAD, WPAD)],
                dst_ref=rbuf.at[side, step, pl.ds(p * WPAD, WPAD)],
                send_sem=send_sem.at[side, step, p],
                recv_sem=recv_sem.at[side, step, p],
                device_id=((gx + (1 if side == 0 else nz - 1)) % nz, gy),
                device_id_type=MESH,
            )
            copy.start()
            copies[side, step, p] = copy

    def put(side, step, p, part):
        value = part[piece(p)]
        earlier = copies.get((side, step - 1, p))
        if earlier is not None:
            earlier.wait_recv()
            value = value + rbuf[side, step - 1, piece(p), :].astype(F32)
        sbuf[side, step, piece(p), :] = value.astype(BF16)
        flush()
        waiting.append((side, step, p))

    first = [(0, 2), (1, 0), (0, 3), (1, 1)]
    second = [(0, 0), (1, 2), (0, 1), (1, 3)]
    part = partial(far)
    for side, p in second:
        sbuf[side, 0, piece(p), :] = part[piece(p)].astype(BF16)
    plus, minus = partial(far - 1), partial(1 - far)
    pl.semaphore_wait(barrier, 2)
    waiting += [(side, 0, p) for side, p in second]
    flush()
    for step in range(1, far):
        for side, p in first:
            put(side, step, p, minus if side else plus)
        if step == 1:
            ahead = partial(far - 2)
            flush()
            ahead = (ahead, partial(2 - far))
        for side, p in second:
            put(side, step, p, minus if side else plus)
        if step > 1:
            d = far - step - 1
            ahead = partial(d)
            flush()
            if d > 0:
                ahead = (ahead, partial(-d))
        else:
            flush()
        if step + 1 < far:
            plus, minus = ahead
    own = ahead
    flush()
    sums = [None] * 4
    for p in (2, 0, 3, 1):
        total = own[piece(p)]
        for side in range(2):
            copies[side, far - 1, p].wait_recv()
            total = total + rbuf[side, far - 1, piece(p), :].astype(F32)
        sums[p] = total[:WCOLS]
    out_ref[...] = jnp.concatenate(sums, axis=0)
    for copy in copies.values():
        copy.wait_send()


VMEM = pl.BlockSpec(memory_space=pltpu.VMEM)
SMEM = pl.BlockSpec(memory_space=pltpu.SMEM)
ANY = pl.BlockSpec(memory_space=pl.ANY)


def solution(mesh):
    nz = mesh.shape["gx"]
    copies = 76

    def shards(queries, new_kv, kv_cache, cache_seg, cache_slot, token_seg, pad_mask, sink_logits, out_weight, out_bias):
        new2 = new_kv.reshape(TOK, 128)
        kv2 = kv_cache.reshape(SLOTS, 128)
        tseg = token_seg.reshape(1, TOK)
        pad = pad_mask.reshape(1, TOK)
        cache_out, block, own = pl.pallas_call(
            prep_kernel,
            name="prep",
            out_shape=(
                jax.ShapeDtypeStruct((SLOTS, 128), BF16),
                jax.ShapeDtypeStruct((ROWS, 128), BF16),
                jax.ShapeDtypeStruct((8, SLOTS), F32),
            ),
            in_specs=[VMEM] * 7,
            out_specs=(VMEM,) * 3,
            compiler_params=pltpu.CompilerParams(vmem_limit_bytes=VMEM_LIMIT),
        )(new2, kv2, cache_seg.reshape(1, SLOTS), cache_slot.reshape(1, TOK), tseg, pad, out_weight.T)
        gathered, qa, state = pl.pallas_call(
            lambda *refs: gather_kernel(copies, *refs),
            name="gather",
            out_shape=(
                jax.ShapeDtypeStruct((NBLK, ROWS, 128), BF16),
                jax.ShapeDtypeStruct((8 * TOK, 128), BF16),
                jax.ShapeDtypeStruct((8 * TOK, 128), F32),
            ),
            in_specs=[SMEM, VMEM, VMEM, VMEM, VMEM, VMEM],
            out_specs=(ANY,) * 3,
            scratch_shapes=[
                pltpu.VMEM((8 * TOK, 128), BF16),
                pltpu.VMEM((8 * TOK, 128), F32),
                pltpu.SemaphoreType.DMA,
                pltpu.SemaphoreType.DMA((2,)),
                pltpu.SemaphoreType.DMA((copies,)),
                pltpu.SemaphoreType.DMA((copies,)),
            ],
            compiler_params=pltpu.CompilerParams(
                collective_id=0, has_side_effects=True, vmem_limit_bytes=VMEM_LIMIT
            ),
        )(sink_logits, queries, cache_out, own, tseg, block)
        attention = pl.pallas_call(
            attend_kernel,
            name="attend",
            out_shape=jax.ShapeDtypeStruct((TOK, 512), BF16),
            in_specs=[SMEM, VMEM, ANY, ANY, ANY],
            out_specs=VMEM,
            scratch_shapes=[
                pltpu.VMEM((NBLK, SLOTS + 80, 128), BF16),
                pltpu.VMEM((NBLK, META, 128), BF16),
                pltpu.VMEM((NBLK * SLOTS + CHUNK + 128, 128), BF16),
                pltpu.VMEM((NBLK * SLOTS + CHUNK + 128, 128), BF16),
                pltpu.VMEM((8 * TOK, 128), BF16),
                pltpu.VMEM((8 * TOK, 128), F32),
                pltpu.VMEM((8 * TOK, 128), F32),
                pltpu.VMEM((NBLK, 128), jnp.int32),
                pltpu.SMEM((NBLK, 128), jnp.int32),
                pltpu.VMEM((NBLK, 128), jnp.int32),
                pltpu.VMEM((NBLK, 128), jnp.int32),
                pltpu.SemaphoreType.DMA((4 + LOADS,)),
            ],
            compiler_params=pltpu.CompilerParams(vmem_limit_bytes=VMEM_LIMIT),
        )(token_seg, pad, qa, state, gathered)
        projected = pl.pallas_call(
            lambda *refs: project_kernel(nz, *refs),
            name="project",
            out_shape=jax.ShapeDtypeStruct((4 * WCOLS, TOK), F32),
            in_specs=[VMEM, ANY],
            out_specs=VMEM,
            scratch_shapes=[
                pltpu.VMEM((NBLK, WROWS, 128), BF16),
                pltpu.VMEM((2, nz // 2, WROWS, TOK), BF16),
                pltpu.VMEM((2, nz // 2, WROWS, TOK), BF16),
                pltpu.SemaphoreType.DMA((nz,)),
                pltpu.SemaphoreType.DMA((2, nz // 2, 4)),
                pltpu.SemaphoreType.DMA((2, nz // 2, 4)),
            ],
            compiler_params=pltpu.CompilerParams(
                collective_id=1, has_side_effects=True, vmem_limit_bytes=VMEM_LIMIT
            ),
        )(attention, gathered)
        attended = (projected.T + out_bias).astype(BF16)
        return attended, cache_out.reshape(SLOTS, 1, 128)

    placed = (
        P("gy", "gx"),
        P("gy", "gx", None),
        P("gy", "gx", None),
        P("gy"),
        P("gy"),
        P("gy"),
        P("gy"),
        P("gx"),
        P("gx", "gy"),
        P("gx"),
    )
    return jax.shard_map(
        shards,
        mesh=mesh,
        in_specs=placed,
        out_specs=(P("gy", "gx"), P("gy", "gx", None)),
        check_vma=False,
    )
```
